32 devices in a mesh: ens: 2 (over y), gy: 4 (over z), gx: 4 (over x, core).
Axes of the slice: x: 2, y: 2, z: 4, core: 2. Of those that a mesh axis runs over, the one named last changes fastest.
Arguments:
- base_stream: float32 [4, 32, 512], P('ens', 'gy', 'gx'), parts along dimension 0, may hold values from -6 to 6
- tangent_vectors: float32 [64, 2, 32, 512], P('ens', None, 'gy', 'gx'), parts along dimension 0, may hold values from -40 to 40, as said below
Outputs:
- basis_vectors: float32 [64, 2, 32, 512], P('ens', None, 'gy', 'gx'), parts along dimension 0
- upper_factor: float32 [64, 32], P('ens'), parts along dimension 0
The draws below stay inside these ranges and needn't reach their ends.
There are 2 independent parts, one for each index of `ens`. The reference program is written for one: setup_inputs(seed, part) draws one part's arguments, and reference() takes and returns one part's arrays. A program takes and returns all parts, laid end to end along the dimension named above; each array names one. Nothing has to cross between parts.
Inputs may be any that keep to these rules, and one draw needn't show every extreme that they name: `tangent_vectors`: Real-valued; the vectors are linearly independent.
All inputs are finite; a program needn't handle non-finite values.
Results may differ from the reference program's by a relative error of at most 0.0003.
Values sent between devices are 32-bit elements; how exact they have to be, the bound alone decides.
No kernel may reach another device: no remote copies, remote signals or barrier semaphores. Data moves between devices by JAX's collectives and lax.ppermute only.
A program may use at most 64 MiB of HBM per device.

```python
import math
import jax
import jax.numpy as jnp
from jax import lax

K = 32
LAYERS = 2
STEPS = 1
NY = 32
NX = 512


def draw_tangent_vectors(key, part):
    first_key, second_key, third_key = jax.random.split(jax.random.fold_in(key, 7), 3)
    noise = jax.random.truncated_normal(first_key, -3.0, 3.0, (K, LAYERS, NY, NX), jnp.float32)
    spread = jax.random.uniform(second_key, (LAYERS, NY, NX), jnp.float32, 0.0, math.log(10.0))
    mixing = 0.4
    upper = jnp.triu(jax.random.uniform(third_key, (K, K), jnp.float32, -1.0, 1.0), 1)
    matrix = jnp.eye(K, dtype=jnp.float32) + mixing * upper
    mixed = jnp.dot(matrix.T, noise.reshape(K, -1), precision=lax.Precision.HIGHEST, preferred_element_type=jnp.float32)
    mixed = mixed.reshape(K, LAYERS, NY, NX) * jnp.exp(spread)
    return jnp.clip(mixed, -40.0, 40.0)


def levels(own_key, shape, shards, least, high):
    def one(axis_at, shards_of):
        steps = jax.random.uniform(jax.random.fold_in(jax.random.fold_in(own_key, 6), axis_at), (shards_of,), jnp.float32, least / len(shards), high / len(shards))
        return jnp.repeat(jnp.exp(steps), shape[axis_at] // shards_of).reshape((-1,) + (1,) * (len(shape) - axis_at - 1))

    factor_of = one(*shards[0])
    for cut in shards[1:]:
        factor_of = factor_of * one(*cut)
    return factor_of


def centred(key, dims, scale, most, cuts=(), kind=jnp.bfloat16):
    values = scale * jax.random.normal(key, dims, jnp.float32)
    if cuts:
        values = values * levels(key, dims, cuts, -0.22, 0.18)
    return jnp.clip(values, -most, most).astype(kind)


def setup_inputs(seed: int = 0, part: int = 0) -> dict:
    streams_of = jax.random.split(jax.random.key(seed), 3)
    own_keys = jax.random.split(jax.random.fold_in(streams_of[2], part), 3)
    base_stream = centred(own_keys[0], (LAYERS, NY, NX), 1.0, 6.0, ((1, 4), (2, 4)), jnp.float32)
    tangent_vectors = draw_tangent_vectors(jax.random.fold_in(jax.random.fold_in(streams_of[2], part), 71), part)
    return {"base_stream": base_stream, "tangent_vectors": tangent_vectors}


coupling_top = 0.6
coupling_bottom = 0.3
time_step = 0.05
hyper_visc = 0.1

def neighbours(values):
    return jnp.roll(values, 1, -1) + jnp.roll(values, -1, -1) + jnp.roll(values, 1, -2) + jnp.roll(values, -1, -2)

def laplacian(values):
    return neighbours(values) - 4.0 * values

def coupling_of(values):
    return jnp.array([coupling_top, coupling_bottom], values.dtype).reshape(2, 1, 1)

def flipped(values):
    return jnp.flip(values, -3)

def delta_cols(values):
    return jnp.roll(values, -1, -1) - jnp.roll(values, 1, -1)

def delta_rows(values):
    return jnp.roll(values, -1, -2) - jnp.roll(values, 1, -2)

def jacobian(first, second):
    return (delta_cols(first) * delta_rows(second) - delta_rows(first) * delta_cols(second)) * 0.25

def relax(stream, potential):
    coupling = coupling_of(potential)
    return (neighbours(stream) + coupling * flipped(stream) - potential) / (4.0 + coupling)

def advance(potential, base_stream, base_pv):
    stream = jnp.zeros_like(potential)
    for section in range(STEPS):
        stream = relax(stream, potential)
        stream = relax(stream, potential)
        tendency = -jacobian(base_stream, potential) - jacobian(stream, base_pv) - hyper_visc * laplacian(laplacian(potential))
        potential = potential + time_step * tendency
    return potential

def reference(base_stream, tangent_vectors):
    coupling = coupling_of(base_stream)
    base_pv = laplacian(base_stream) - coupling * (base_stream - flipped(base_stream))
    evolved = lax.map(lambda vector: advance(vector, base_stream, base_pv), tangent_vectors)
    columns = evolved.reshape(K, -1)
    total = 2.0 * NY * NX
    gram = jnp.dot(columns.astype(jnp.float32), columns.T.astype(jnp.float32), precision=lax.Precision.HIGHEST, preferred_element_type=jnp.float32) / total
    lower = jnp.linalg.cholesky(gram)
    basis = lax.linalg.triangular_solve(lower, columns, left_side=True, lower=True)
    return (basis.reshape(evolved.shape), lower.T)
```

```python
import jax
import jax.numpy as jnp
from jax import lax
from jax.experimental import pallas as pl
from jax.experimental.pallas import tpu as pltpu
from jax.sharding import PartitionSpec as P

coupling_pair = (0.6, 0.3)
time_step = 0.05
hyper_visc = 0.1

SUB = 8
VMEM = pl.BlockSpec(memory_space=pltpu.VMEM)


def pairings(value_a, value_b, axis):
    count = lax.axis_size(axis)
    got_b = lax.ppermute(value_b, axis, [(i, (i + 1 if i % 2 else i - 1) % count) for i in range(count)])
    got_a = lax.ppermute(value_a, axis, [(i, (i + 1 if i % 2 == 0 else i - 1) % count) for i in range(count)])
    return got_a, got_b


def is_even(axis):
    return lax.rem(lax.axis_index(axis), 2) == 0


def lanes_of(shape):
    return lax.broadcasted_iota(jnp.int32, shape, len(shape) - 1)


class Rows:
    def __init__(self, sizes, pv, base, got_a, got_b):
        self.vectors, self.layers, self.rows, self.columns = sizes
        self.groups = self.vectors // SUB
        self.pv, self.base, self.got_a, self.got_b = pv, base, got_a, got_b
        self.even = is_even("gy")

    def halo(self, side, layer, step, group):
        if group < self.groups:
            at = pl.ds((layer * 2 + step) * self.vectors + group * SUB, SUB)
        else:
            at = pl.ds(self.layers * 2 * self.vectors + layer * 2 + step, 1)
        first, second = self.got_a[at, :], self.got_b[at, :]
        found = jnp.where(self.even, second, first) if side == "above" else jnp.where(self.even, first, second)
        return jnp.broadcast_to(found, (SUB, self.columns))

    def own(self, layer, row, group):
        if group < self.groups:
            stride = self.layers * self.rows
            return self.pv[pl.ds(group * SUB * stride + layer * self.rows + row, SUB, stride=stride), :]
        return jnp.broadcast_to(self.base[pl.ds(layer * self.rows + row, 1), :], (SUB, self.columns))

    def get(self, layer, row, group):
        if row < 0:
            return self.halo("above", layer, row + 2, group)
        if row >= self.rows:
            return self.halo("below", layer, row - self.rows, group)
        return self.own(layer, row, group)


def pack_rows_body(sizes, pv, base, out_a, out_b):
    vectors, layers, rows, columns = sizes
    source = Rows(sizes, pv, base, None, None)
    for layer in range(layers):
        for step in range(2):
            for group in range(source.groups + 1):
                top = source.own(layer, step, group)
                bottom = source.own(layer, rows - 2 + step, group)
                if group < source.groups:
                    at = pl.ds((layer * 2 + step) * vectors + group * SUB, SUB)
                else:
                    at = pl.ds(layers * 2 * vectors + layer * 2 + step, 1)
                    top, bottom = top[:1], bottom[:1]
                out_a[at, :] = jnp.where(source.even, bottom, top)
                out_b[at, :] = jnp.where(source.even, top, bottom)
    left = pl.ds(layers * 2 * (vectors + 1), SUB - layers * 2)
    out_a[left, :] = jnp.zeros((SUB - layers * 2, columns), jnp.float32)
    out_b[left, :] = jnp.zeros((SUB - layers * 2, columns), jnp.float32)


def pack_columns_body(sizes, pv, base, got_a, got_b, out):
    vectors, layers, rows, columns = sizes
    source = Rows(sizes, pv, base, got_a, got_b)
    spot = lanes_of((SUB, columns)) // 4
    for group in range(source.groups + 1):
        total = jnp.zeros((SUB, columns), jnp.float32)
        for layer in range(layers):
            for row in range(-1, rows + 1):
                place = layer * (rows + 2) + row + 1
                turned = pltpu.roll(source.get(layer, row, group), (2 + 4 * place) % columns, 1)
                total = jnp.where(spot == place, turned, total)
        out[pl.ds(group * SUB, SUB), :] = total


def stencil_body(sizes, scale, pv, base, got_a, got_b, side_a, side_b, evolved, gram, coef):
    vectors, layers, rows, columns = sizes
    source = Rows(sizes, pv, base, got_a, got_b)
    lane = lanes_of((SUB, columns))
    from_a = jnp.logical_xor(lax.rem(lane, 4) < 2, is_even("gx"))

    def fields(group):
        block = pl.ds(group * SUB, SUB)
        sides = jnp.where(from_a, side_a[block, :], side_b[block, :])
        value, dx, sx, dx2, sx2 = {}, {}, {}, {}, {}
        for layer in range(layers):
            for row in range(-2, rows + 2):
                here = source.get(layer, row, group)
                value[layer, row] = here
                if row == -2 or row == rows + 1:
                    continue
                place = layer * (rows + 2) + row + 1
                edge = pltpu.roll(sides, (columns - 2 - 4 * place) % columns, 1)
                left, right = jnp.where(lane == columns - 1, edge, here), jnp.where(lane == 0, edge, here)
                west, east = pltpu.roll(left, 1, 1), pltpu.roll(right, columns - 1, 1)
                dx[layer, row], sx[layer, row] = east - west, east + west
                if 0 <= row < rows:
                    left, right = jnp.where(lane >= columns - 2, edge, here), jnp.where(lane < 2, edge, here)
                    west, east = pltpu.roll(left, 2, 1), pltpu.roll(right, columns - 2, 1)
                    dx2[layer, row], sx2[layer, row] = east - west, east + west
        dy, near, near_dx, near_dy = {}, {}, {}, {}
        for layer in range(layers):
            for row in range(rows):
                k = (layer, row)
                up, down = (layer, row - 1), (layer, row + 1)
                dy[k] = value[down] - value[up]
                near[k] = sx[k] + (value[down] + value[up])
                near_dx[k] = dx2[k] + (dx[down] + dx[up])
                near_dy[k] = (sx[down] - sx[up]) + (value[layer, row + 2] - value[layer, row - 2])
        return value, dx, sx, sx2, dy, near, near_dx, near_dy

    other = lambda layer: layers - 1 - layer
    value, dx, sx, sx2, dy, near, near_dx, near_dy = fields(source.groups)
    for layer in range(layers):
        c, c_other = coupling_pair[layer], coupling_pair[other(layer)]
        a = 1.0 / (4.0 + c)
        for row in range(rows):
            k, o = (layer, row), (other(layer), row)
            base_dx, base_dy = dx[k], dy[k]
            pv_dx = near_dx[k] - (4.0 + c) * base_dx + c * dx[o]
            pv_dy = near_dy[k] - (4.0 + c) * base_dy + c * dy[o]
            j = 0.25 * time_step
            coef[layer * rows + row, 0] = j * (base_dy + a * pv_dy)
            coef[layer * rows + row, 1] = -j * (base_dx + a * pv_dx)
            coef[layer * rows + row, 2] = (j * a * a) * pv_dy
            coef[layer * rows + row, 3] = (-j * a * a) * pv_dx
    v = time_step * hyper_visc
    for group in range(source.groups):
        value, dx, sx, sx2, dy, near, near_dx, near_dy = fields(group)
        for layer in range(layers):
            c, c_other = coupling_pair[layer], coupling_pair[other(layer)]
            cross = c * (4.0 + c) / (4.0 + c_other)
            for row in range(rows):
                k, o = (layer, row), (other(layer), row)
                up, down = (layer, row - 1), (layer, row + 1)
                at = layer * rows + row
                diagonal = sx[down] + sx[up]
                far = sx2[k] + (value[layer, row + 2] + value[layer, row - 2])
                result = (1.0 - 20.0 * v) * value[k] + (8.0 * v) * near[k] - (2.0 * v) * diagonal - v * far
                result = result + (coef[at, 0] * dx[k] + coef[at, 1] * dy[k])
                result = result + coef[at, 2] * (near_dx[k] + cross * dx[o])
                result = result + coef[at, 3] * (near_dy[k] + cross * dy[o])
                evolved[pl.ds(group * SUB, SUB), pl.ds(at * columns, columns)] = result
    whole = evolved[...]
    local = lax.dot_general(
        whole, whole, (((1,), (1,)), ((), ())),
        precision=lax.Precision.HIGHEST, preferred_element_type=jnp.float32,
    ) * scale
    gram[...] = jnp.concatenate([local[g * SUB : (g + 1) * SUB] for g in range(source.groups)], axis=1)


def basis_body(sizes, evolved, gram, basis, upper):
    vectors, layers, rows, columns = sizes
    groups = vectors // SUB
    shape = (SUB, columns)
    lane = lanes_of(shape)
    sub = lax.broadcasted_iota(jnp.int32, shape, 0)
    packed = gram[...]
    work = []
    for group in range(groups):
        turned = pltpu.roll(packed, (columns - group * vectors) % columns, 1)
        unit = jnp.where(lane - vectors == sub + group * SUB, 1.0, 0.0)
        work.append(jnp.where(lane < vectors, turned, unit))
    for k in range(vectors):
        home, at = k // SUB, k % SUB
        line = jnp.broadcast_to(work[home][at : at + 1, :], shape)
        pivot = 1.0 / jnp.broadcast_to(line[:, k : k + 1], shape)
        for group in range(home, groups):
            if group == home and at == SUB - 1:
                continue
            factor = jnp.broadcast_to(work[group][:, k : k + 1], shape) * pivot
            if group == home:
                factor = jnp.where(sub > at, factor, 0.0)
            work[group] = work[group] - factor * line
    inverse = []
    for group in range(groups):
        row = sub + group * SUB
        pivot = jnp.sum(jnp.where(lane == row, work[group], 0.0), axis=1, keepdims=True)
        done = work[group] * (1.0 / jnp.sqrt(jnp.broadcast_to(pivot, shape)))
        upper[pl.ds(group * SUB, SUB), :] = jnp.where(lane >= row, done, 0.0)[:, :vectors]
        inverse.append(pltpu.roll(done, columns - vectors, 1)[:, :vectors])
    inverse = jnp.concatenate(inverse, axis=0)
    stride = layers * rows
    for at in range(stride):
        part = jnp.dot(
            inverse, evolved[:, pl.ds(at * columns, columns)],
            precision=lax.Precision.HIGHEST, preferred_element_type=jnp.float32,
        )
        for group in range(groups):
            basis[pl.ds(group * SUB * stride + at, SUB, stride=stride), :] = part[group * SUB : (group + 1) * SUB]


def local(base_stream, tangent_vectors):
    sizes = tangent_vectors.shape
    vectors, layers, rows, columns = sizes
    pv = tangent_vectors.reshape(vectors * layers * rows, columns)
    base = base_stream.reshape(layers * rows, columns)
    f32 = lambda *shape: jax.ShapeDtypeStruct(shape, jnp.float32)

    def call(body, outs, *operands, scratch=()):
        return pl.pallas_call(
            lambda *refs: body(sizes, *refs),
            out_shape=outs,
            in_specs=[VMEM] * len(operands),
            out_specs=[VMEM] * len(outs),
            scratch_shapes=scratch,
            compiler_params=pltpu.CompilerParams(vmem_limit_bytes=8 << 20),
        )(*operands)

    strip = f32(layers * 2 * vectors + SUB, columns)
    row_a, row_b = call(pack_rows_body, [strip, strip], pv, base)
    got_a, got_b = pairings(row_a, row_b, "gy")
    (side,) = call(pack_columns_body, [f32(vectors + SUB, columns)], pv, base, got_a, got_b)
    side_a, side_b = pairings(side, side, "gx")
    cells = layers * rows * columns
    tiles = lax.axis_size("gy") * lax.axis_size("gx")
    scale = 1.0 / (cells * tiles)
    evolved, gram = call(
        lambda sizes, *refs: stencil_body(sizes, scale, *refs),
        [f32(vectors, cells), f32(SUB, vectors * vectors // SUB)],
        pv, base, got_a, got_b, side_a, side_b,
        scratch=[pltpu.VMEM((layers * rows, 4, SUB, columns), jnp.float32)],
    )
    spread = jnp.broadcast_to(gram[None], (tiles,) + gram.shape)
    gram = lax.all_to_all(spread, ("gy", "gx"), 0, 0, tiled=True).sum(0)
    basis, upper = call(
        basis_body, [f32(vectors * layers * rows, columns), f32(vectors, vectors)], evolved, gram
    )
    return basis.reshape(sizes), upper


def solution(mesh):
    return jax.shard_map(
        local,
        mesh=mesh,
        in_specs=(P("ens", "gy", "gx"), P("ens", None, "gy", "gx")),
        out_specs=(P("ens", None, "gy", "gx"), P("ens", None)),
        check_vma=False,
    )
```

```python
import jax
import jax.numpy as jnp
from jax import lax
from jax.experimental import pallas as pl
from jax.experimental.pallas import tpu as pltpu
from jax.sharding import PartitionSpec as P

coupling_pair = (0.6, 0.3)
time_step = 0.05
hyper_visc = 0.1

SUB = 8
VMEM = pl.BlockSpec(memory_space=pltpu.VMEM)


def pairings(value_a, value_b, axis):
    count = lax.axis_size(axis)
    got_b = lax.ppermute(value_b, axis, [(i, (i + 1 if i % 2 else i - 1) % count) for i in range(count)])
    got_a = lax.ppermute(value_a, axis, [(i, (i + 1 if i % 2 == 0 else i - 1) % count) for i in range(count)])
    return got_a, got_b


def is_even(axis):
    return lax.rem(lax.axis_index(axis), 2) == 0


def lanes_of(shape):
    return lax.broadcasted_iota(jnp.int32, shape, len(shape) - 1)


class Rows:
    def __init__(self, sizes, pv, base, got_a, got_b):
        self.vectors, self.layers, self.rows, self.columns = sizes
        self.groups = self.vectors // SUB
        self.pv, self.base, self.got_a, self.got_b = pv, base, got_a, got_b
        self.even = is_even("gy")

    def halo(self, side, layer, step, group):
        if group < self.groups:
            at = pl.ds((layer * 2 + step) * self.vectors + group * SUB, SUB)
        else:
            at = pl.ds(self.layers * 2 * self.vectors + layer * 2 + step, 1)
        first, second = self.got_a[at, :], self.got_b[at, :]
        found = jnp.where(self.even, second, first) if side == "above" else jnp.where(self.even, first, second)
        return jnp.broadcast_to(found, (SUB, self.columns))

    def own(self, layer, row, group):
        if group < self.groups:
            stride = self.layers * self.rows
            return self.pv[pl.ds(group * SUB * stride + layer * self.rows + row, SUB, stride=stride), :]
        return jnp.broadcast_to(self.base[pl.ds(layer * self.rows + row, 1), :], (SUB, self.columns))

    def get(self, layer, row, group):
        if row < 0:
            return self.halo("above", layer, row + 2, group)
        if row >= self.rows:
            return self.halo("below", layer, row - self.rows, group)
        return self.own(layer, row, group)


def pack_rows_body(sizes, pv, base, out_a, out_b, pv_rows, base_rows, done):
    vectors, layers, rows, columns = sizes
    ends = (0, rows - 2)
    copies = [
        pltpu.make_async_copy(pv.at[:, pl.ds(first, 2), :], pv_rows.at[:, pl.ds(first, 2), :], done.at[n])
        for n, first in enumerate(ends)
    ]
    copies.append(pltpu.make_async_copy(base, base_rows, done.at[2]))
    for copy in copies:
        copy.start()
    for copy in copies:
        copy.wait()
    source = Rows(sizes, pv_rows.reshape(vectors * layers * rows, columns), base_rows, None, None)
    for layer in range(layers):
        for step in range(2):
            for group in range(source.groups + 1):
                top = source.own(layer, step, group)
                bottom = source.own(layer, rows - 2 + step, group)
                if group < source.groups:
                    at = pl.ds((layer * 2 + step) * vectors + group * SUB, SUB)
                else:
                    at = pl.ds(layers * 2 * vectors + layer * 2 + step, 1)
                    top, bottom = top[:1], bottom[:1]
                out_a[at, :] = jnp.where(source.even, bottom, top)
                out_b[at, :] = jnp.where(source.even, top, bottom)
    left = pl.ds(layers * 2 * (vectors + 1), SUB - layers * 2)
    out_a[left, :] = jnp.zeros((SUB - layers * 2, columns), jnp.float32)
    out_b[left, :] = jnp.zeros((SUB - layers * 2, columns), jnp.float32)


def pack_columns_body(sizes, pv, base, got_a, got_b, out):
    vectors, layers, rows, columns = sizes
    source = Rows(sizes, pv, base, got_a, got_b)
    spot = lanes_of((SUB, columns)) // 4
    for group in range(source.groups + 1):
        total = jnp.zeros((SUB, columns), jnp.float32)
        for layer in range(layers):
            for row in range(-1, rows + 1):
                place = layer * (rows + 2) + row + 1
                turned = pltpu.roll(source.get(layer, row, group), (2 + 4 * place) % columns, 1)
                total = jnp.where(spot == place, turned, total)
        out[pl.ds(group * SUB, SUB), :] = total


def stencil_body(sizes, scale, pv, base, got_a, got_b, side_a, side_b, evolved, gram, coef):
    vectors, layers, rows, columns = sizes
    source = Rows(sizes, pv, base, got_a, got_b)
    lane = lanes_of((SUB, columns))
    from_a = jnp.logical_xor(lax.rem(lane, 4) < 2, is_even("gx"))

    def fields(group):
        block = pl.ds(group * SUB, SUB)
        sides = jnp.where(from_a, side_a[block, :], side_b[block, :])
        value, dx, sx, dx2, sx2 = {}, {}, {}, {}, {}
        for layer in range(layers):
            for row in range(-2, rows + 2):
                here = source.get(layer, row, group)
                value[layer, row] = here
                if row == -2 or row == rows + 1:
                    continue
                place = layer * (rows + 2) + row + 1
                edge = pltpu.roll(sides, (columns - 2 - 4 * place) % columns, 1)
                left, right = jnp.where(lane == columns - 1, edge, here), jnp.where(lane == 0, edge, here)
                west, east = pltpu.roll(left, 1, 1), pltpu.roll(right, columns - 1, 1)
                dx[layer, row], sx[layer, row] = east - west, east + west
                if 0 <= row < rows:
                    left, right = jnp.where(lane >= columns - 2, edge, here), jnp.where(lane < 2, edge, here)
                    west, east = pltpu.roll(left, 2, 1), pltpu.roll(right, columns - 2, 1)
                    dx2[layer, row], sx2[layer, row] = east - west, east + west
        dy, near, near_dx, near_dy = {}, {}, {}, {}
        for layer in range(layers):
            for row in range(rows):
                k = (layer, row)
                up, down = (layer, row - 1), (layer, row + 1)
                dy[k] = value[down] - value[up]
                near[k] = sx[k] + (value[down] + value[up])
                near_dx[k] = dx2[k] + (dx[down] + dx[up])
                near_dy[k] = (sx[down] - sx[up]) + (value[layer, row + 2] - value[layer, row - 2])
        return value, dx, sx, sx2, dy, near, near_dx, near_dy

    other = lambda layer: layers - 1 - layer
    value, dx, sx, sx2, dy, near, near_dx, near_dy = fields(source.groups)
    for layer in range(layers):
        c, c_other = coupling_pair[layer], coupling_pair[other(layer)]
        a = 1.0 / (4.0 + c)
        for row in range(rows):
            k, o = (layer, row), (other(layer), row)
            base_dx, base_dy = dx[k], dy[k]
            pv_dx = near_dx[k] - (4.0 + c) * base_dx + c * dx[o]
            pv_dy = near_dy[k] - (4.0 + c) * base_dy + c * dy[o]
            j = 0.25 * time_step
            coef[layer * rows + row, 0] = j * (base_dy + a * pv_dy)
            coef[layer * rows + row, 1] = -j * (base_dx + a * pv_dx)
            coef[layer * rows + row, 2] = (j * a * a) * pv_dy
            coef[layer * rows + row, 3] = (-j * a * a) * pv_dx
    v = time_step * hyper_visc
    for group in range(source.groups):
        value, dx, sx, sx2, dy, near, near_dx, near_dy = fields(group)
        for layer in range(layers):
            c, c_other = coupling_pair[layer], coupling_pair[other(layer)]
            cross = c * (4.0 + c) / (4.0 + c_other)
            for row in range(rows):
                k, o = (layer, row), (other(layer), row)
                up, down = (layer, row - 1), (layer, row + 1)
                at = layer * rows + row
                diagonal = sx[down] + sx[up]
                far = sx2[k] + (value[layer, row + 2] + value[layer, row - 2])
                result = (1.0 - 20.0 * v) * value[k] + (8.0 * v) * near[k] - (2.0 * v) * diagonal - v * far
                result = result + (coef[at, 0] * dx[k] + coef[at, 1] * dy[k])
                result = result + coef[at, 2] * (near_dx[k] + cross * dx[o])
                result = result + coef[at, 3] * (near_dy[k] + cross * dy[o])
                evolved[pl.ds(group * SUB, SUB), pl.ds(at * columns, columns)] = result
    whole = evolved[...]
    local = lax.dot_general(
        whole, whole, (((1,), (1,)), ((), ())),
        precision=lax.Precision.HIGHEST, preferred_element_type=jnp.float32,
    ) * scale
    gram[...] = jnp.concatenate([local[g * SUB : (g + 1) * SUB] for g in range(source.groups)], axis=1)


def basis_body(sizes, evolved, gram, basis, upper):
    vectors, layers, rows, columns = sizes
    groups = vectors // SUB
    shape = (SUB, columns)
    lane = lanes_of(shape)
    sub = lax.broadcasted_iota(jnp.int32, shape, 0)
    packed = gram[...]
    work = []
    for group in range(groups):
        turned = pltpu.roll(packed, (columns - group * vectors) % columns, 1)
        unit = jnp.where(lane - vectors == sub + group * SUB, 1.0, 0.0)
        work.append(jnp.where(lane < vectors, turned, unit))
    for home in range(groups):
        first = home * SUB
        column = {
            (group, j): jnp.broadcast_to(work[group][:, first + j : first + j + 1], shape)
            for group in range(home, groups)
            for j in range(SUB)
        }
        for at in range(SUB):
            inverse_pivot = jnp.broadcast_to((1.0 / column[home, at])[at : at + 1, :], shape)
            line = jnp.broadcast_to(work[home][at : at + 1, :], shape)
            for group in range(home, groups):
                factor = column[group, at] * inverse_pivot
                if group == home:
                    factor = jnp.where(sub > at, factor, 0.0)
                for j in range(at + 1, SUB):
                    level = jnp.broadcast_to(column[home, j][at : at + 1, :], shape)
                    if group == home:
                        column[home, j, "next"] = column[home, j] - factor * level
                    else:
                        column[group, j] = column[group, j] - factor * level
                work[group] = work[group] - factor * line
            for j in range(at + 1, SUB):
                column[home, j] = column.pop((home, j, "next"))
    inverse = []
    for group in range(groups):
        row = sub + group * SUB
        pivot = jnp.sum(jnp.where(lane == row, work[group], 0.0), axis=1, keepdims=True)
        done = work[group] * (1.0 / jnp.sqrt(jnp.broadcast_to(pivot, shape)))
        upper[pl.ds(group * SUB, SUB), :] = jnp.where(lane >= row, done, 0.0)[:, :vectors]
        inverse.append(pltpu.roll(done, columns - vectors, 1)[:, :vectors])
    inverse = jnp.concatenate(inverse, axis=0)
    stride = layers * rows
    wide = 2 if stride % 2 == 0 else 1
    for first in range(0, stride, wide):
        part = jnp.dot(
            inverse, evolved[:, pl.ds(first * columns, wide * columns)],
            precision=lax.Precision.HIGHEST, preferred_element_type=jnp.float32,
        )
        for n in range(wide):
            for group in range(groups):
                at = pl.ds(group * SUB * stride + first + n, SUB, stride=stride)
                basis[at, :] = part[group * SUB : (group + 1) * SUB, n * columns : (n + 1) * columns]


def local(base_stream, tangent_vectors):
    sizes = tangent_vectors.shape
    vectors, layers, rows, columns = sizes
    pv = tangent_vectors.reshape(vectors * layers * rows, columns)
    base = base_stream.reshape(layers * rows, columns)
    f32 = lambda *shape: jax.ShapeDtypeStruct(shape, jnp.float32)

    def call(body, outs, *operands, scratch=(), inputs=VMEM):
        return pl.pallas_call(
            lambda *refs: body(sizes, *refs),
            out_shape=outs,
            in_specs=[inputs] * len(operands),
            out_specs=[VMEM] * len(outs),
            scratch_shapes=scratch,
            compiler_params=pltpu.CompilerParams(vmem_limit_bytes=8 << 20),
        )(*operands)

    strip = f32(layers * 2 * vectors + SUB, columns)
    row_a, row_b = call(
        pack_rows_body, [strip, strip],
        pltpu.with_memory_space_constraint(tangent_vectors.reshape(vectors * layers, rows, columns), pltpu.HBM),
        pltpu.with_memory_space_constraint(base, pltpu.HBM),
        inputs=pl.BlockSpec(memory_space=pltpu.HBM),
        scratch=[
            pltpu.VMEM((vectors * layers, rows, columns), jnp.float32),
            pltpu.VMEM((layers * rows, columns), jnp.float32),
            pltpu.SemaphoreType.DMA((3,)),
        ],
    )
    got_a, got_b = pairings(row_a, row_b, "gy")
    (side,) = call(pack_columns_body, [f32(vectors + SUB, columns)], pv, base, got_a, got_b)
    side_a, side_b = pairings(side, side, "gx")
    cells = layers * rows * columns
    tiles = lax.axis_size("gy") * lax.axis_size("gx")
    scale = 1.0 / (cells * tiles)
    evolved, gram = call(
        lambda sizes, *refs: stencil_body(sizes, scale, *refs),
        [f32(vectors, cells), f32(SUB, vectors * vectors // SUB)],
        pv, base, got_a, got_b, side_a, side_b,
        scratch=[pltpu.VMEM((layers * rows, 4, SUB, columns), jnp.float32)],
    )
    spread = jnp.broadcast_to(gram[None], (tiles,) + gram.shape)
    gram = lax.all_to_all(spread, ("gy", "gx"), 0, 0, tiled=True).sum(0)
    basis, upper = call(
        basis_body, [f32(vectors * layers * rows, columns), f32(vectors, vectors)], evolved, gram
    )
    return basis.reshape(sizes), upper


def solution(mesh):
    return jax.shard_map(
        local,
        mesh=mesh,
        in_specs=(P("ens", "gy", "gx"), P("ens", None, "gy", "gx")),
        out_specs=(P("ens", None, "gy", "gx"), P("ens", None)),
        check_vma=False,
    )
```

```python
import jax
import jax.numpy as jnp
from jax import lax
from jax.experimental import pallas as pl
from jax.experimental.pallas import tpu as pltpu
from jax.sharding import PartitionSpec as P

coupling_pair = (0.6, 0.3)
time_step = 0.05
hyper_visc = 0.1

SUB = 8
EDGE = 4
SPAN = 2 * EDGE
VMEM = pl.BlockSpec(memory_space=pltpu.VMEM)


def lanes_of(shape):
    return lax.broadcasted_iota(jnp.int32, shape, len(shape) - 1)


class Rows:
    def __init__(self, sizes, pv, base, above, below):
        self.vectors, self.layers, self.rows, self.columns = sizes
        self.groups = self.vectors // SUB
        self.pv, self.base, self.above, self.below = pv, base, above, below

    def halo(self, strip, layer, step, group):
        if group < self.groups:
            return strip[pl.ds((layer * 2 + step) * self.vectors + group * SUB, SUB), :]
        found = strip[pl.ds(self.layers * 2 * self.vectors + layer * 2 + step, 1), :]
        return jnp.broadcast_to(found, (SUB, self.columns))

    def own(self, layer, row, group):
        if group < self.groups:
            stride = self.layers * self.rows
            return self.pv[pl.ds(group * SUB * stride + layer * self.rows + row, SUB, stride=stride), :]
        return jnp.broadcast_to(self.base[pl.ds(layer * self.rows + row, 1), :], (SUB, self.columns))

    def get(self, layer, row, group):
        if row < 0:
            return self.halo(self.above, layer, row + 2, group)
        if row >= self.rows:
            return self.halo(self.below, layer, row - self.rows, group)
        return self.own(layer, row, group)


def pack_rows_body(sizes, pv, base, bottom, top, pv_rows, base_rows, done):
    vectors, layers, rows, columns = sizes
    ends = (0, rows - 2)
    copies = [
        pltpu.make_async_copy(pv.at[:, pl.ds(first, 2), :], pv_rows.at[:, pl.ds(first, 2), :], done.at[n])
        for n, first in enumerate(ends)
    ]
    copies.append(pltpu.make_async_copy(base, base_rows, done.at[2]))
    for copy in copies:
        copy.start()
    for copy in copies:
        copy.wait()
    source = Rows(sizes, pv_rows.reshape(vectors * layers * rows, columns), base_rows, None, None)
    for out, first in ((top, 0), (bottom, rows - 2)):
        for layer in range(layers):
            for step in range(2):
                for group in range(source.groups):
                    at = pl.ds((layer * 2 + step) * vectors + group * SUB, SUB)
                    out[at, :] = source.own(layer, first + step, group)
                at = pl.ds(layers * 2 * vectors + layer * 2 + step, 1)
                out[at, :] = source.own(layer, first + step, source.groups)[:1]
        out[pl.ds(layers * 2 * (vectors + 1), SUB - layers * 2), :] = jnp.zeros((SUB - layers * 2, columns), jnp.float32)


class Fields:
    pass


def base_weights(at, other, layer):
    c = coupling_pair[layer]
    a = 1.0 / (4.0 + c)
    j = 0.25 * time_step
    pv_dx = at.near_dx - (4.0 + c) * at.dx + c * other.dx
    pv_dy = at.near_dy - (4.0 + c) * at.dy + c * other.dy
    return (
        j * (at.dy + a * pv_dy),
        -j * (at.dx + a * pv_dx),
        (j * a * a) * pv_dy,
        (-j * a * a) * pv_dx,
    )


def stepped(at, other, layer, weights):
    c, c_other = coupling_pair[layer], coupling_pair[1 - layer]
    cross = c * (4.0 + c) / (4.0 + c_other)
    v = time_step * hyper_visc
    result = (1.0 - 20.0 * v) * at.value + (8.0 * v) * at.near - (2.0 * v) * at.diagonal - v * at.far
    result = result + (weights[0] * at.dx + weights[1] * at.dy)
    result = result + weights[2] * (at.near_dx + cross * other.dx)
    return result + weights[3] * (at.near_dy + cross * other.dy)


def packed_gram(whole, scale):
    local = lax.dot_general(
        whole, whole, (((1,), (1,)), ((), ())),
        precision=lax.Precision.HIGHEST, preferred_element_type=jnp.float32,
    ) * scale
    return jnp.concatenate([local[at : at + SUB] for at in range(0, whole.shape[0], SUB)], axis=1)


def stencil_body(sizes, scale, pv, base, above, below, evolved, message, coef):
    vectors, layers, rows, columns = sizes
    source = Rows(sizes, pv, base, above, below)
    lane = lanes_of((SUB, columns))
    inside = jnp.logical_and(lane >= 2, lane < columns - 2)
    place = lane // SPAN

    def fields(group):
        value, dx, sx, dx2, sx2 = {}, {}, {}, {}, {}
        for layer in range(layers):
            edges = jnp.zeros((SUB, columns), jnp.float32)
            for row in range(-2, rows + 2):
                here = source.get(layer, row, group)
                value[layer, row] = here
                turned = pltpu.roll(here, (EDGE + SPAN * (row + 2)) % columns, 1)
                edges = jnp.where(place == row + 2, turned, edges)
                if row == -2 or row == rows + 1:
                    continue
                west, east = pltpu.roll(here, 1, 1), pltpu.roll(here, columns - 1, 1)
                dx[layer, row], sx[layer, row] = east - west, east + west
                if 0 <= row < rows:
                    west, east = pltpu.roll(here, 2, 1), pltpu.roll(here, columns - 2, 1)
                    dx2[layer, row], sx2[layer, row] = east - west, east + west
            message[pl.ds(SUB + layer * (vectors + SUB) + group * SUB, SUB), :] = edges
        found = {}
        for layer in range(layers):
            for row in range(rows):
                up, down = (layer, row - 1), (layer, row + 1)
                at = found[layer, row] = Fields()
                at.value, at.dx = value[layer, row], dx[layer, row]
                at.dy = value[down] - value[up]
                at.near = sx[layer, row] + (value[down] + value[up])
                at.near_dx = dx2[layer, row] + (dx[down] + dx[up])
                at.near_dy = (sx[down] - sx[up]) + (value[layer, row + 2] - value[layer, row - 2])
                at.diagonal = sx[down] + sx[up]
                at.far = sx2[layer, row] + (value[layer, row + 2] + value[layer, row - 2])
        return found

    found = fields(source.groups)
    for layer in range(layers):
        for row in range(rows):
            for n, weight in enumerate(base_weights(found[layer, row], found[1 - layer, row], layer)):
                coef[layer * rows + row, n] = weight
    for group in range(source.groups):
        found = fields(group)
        for layer in range(layers):
            for row in range(rows):
                at = layer * rows + row
                weights = [coef[at, n] for n in range(4)]
                result = stepped(found[layer, row], found[1 - layer, row], layer, weights)
                evolved[pl.ds(group * SUB, SUB), pl.ds(at * columns, columns)] = jnp.where(inside, result, 0.0)
    message[pl.ds(0, SUB), :] = packed_gram(evolved[...], scale)


def strip_fields(here, columns):
    turn = lambda value, by: pltpu.roll(value, by % columns, 1)
    at = Fields()
    west, east = turn(here, 1), turn(here, -1)
    at.value, at.dx, sx = here, east - west, east + west
    west, east = turn(here, 2), turn(here, -2)
    dx2, sx2 = east - west, east + west
    up, down = turn(here, SPAN), turn(here, -SPAN)
    at.dy, at.near = down - up, sx + (down + up)
    at.near_dx = dx2 + (turn(at.dx, -SPAN) + turn(at.dx, SPAN))
    far_up, far_down = turn(here, 2 * SPAN), turn(here, -2 * SPAN)
    sx_up, sx_down = turn(sx, SPAN), turn(sx, -SPAN)
    at.near_dy = (sx_down - sx_up) + (far_down - far_up)
    at.diagonal, at.far = sx_down + sx_up, sx2 + (far_down + far_up)
    return at


def join_body(sizes, scale, half, last, *refs):
    vectors, layers, rows, columns = sizes
    refs = list(refs)
    mine, got = refs[:2]
    sides_in = refs[2] if half > 1 else None
    outs = refs[3:] if half > 1 else refs[2:]
    message, sides, strips = outs
    groups = vectors // SUB
    shape = (SUB, columns)
    lane = lanes_of(shape)
    column = lax.rem(lane, SPAN)
    west_half = column < EDGE
    valid = jnp.logical_and(
        jnp.logical_and(column >= 2, column < SPAN - 2),
        jnp.logical_and(lane >= 2 * SPAN, lane < (rows + 2) * SPAN),
    )
    tile = lax.axis_index("gx")
    spot = lax.rem(tile, 2 * half)
    first = spot < half
    mid_mine = jnp.logical_xor(west_half, jnp.logical_not(first))
    keep_mid = jnp.logical_or(jnp.logical_and(west_half, spot == half - 1), jnp.logical_and(~west_half, spot == half))
    keep_wrap = jnp.logical_or(jnp.logical_and(west_half, spot == 2 * half - 1), jnp.logical_and(~west_half, spot == 0))
    kinds = (False, True) if last else (False,)
    weights = {}
    for group in (groups, *range(groups)):
        found = {}
        for layer in range(layers):
            at = pl.ds(SUB + layer * (vectors + SUB) + group * SUB, SUB)
            here, there = mine[at, :], got[at, :]
            mid, outer = jnp.where(mid_mine, here, there), jnp.where(mid_mine, there, here)
            if not last:
                message[at, :] = outer
            found[layer, False] = strip_fields(mid, columns)
            if last:
                found[layer, True] = strip_fields(outer, columns)
        for layer in range(layers):
            own = None
            for wrap in kinds:
                at, other = found[layer, wrap], found[1 - layer, wrap]
                if group == groups:
                    weights[layer, wrap] = base_weights(at, other, layer)
                    continue
                result = jnp.where(valid, stepped(at, other, layer, weights[layer, wrap]), 0.0)
                strips[pl.ds(group * SUB, SUB), pl.ds((layer * len(kinds) + wrap) * columns, columns)] = result
                where = pl.ds(layer * vectors + group * SUB, SUB)
                if own is None:
                    own = sides_in[where, :] if half > 1 else jnp.zeros(shape, jnp.float32)
                own = jnp.where(keep_wrap if wrap else keep_mid, result, own)
                if wrap == last:
                    sides[where, :] = own
    head = pl.ds(0, SUB)
    message[head, :] = (mine[head, :] + got[head, :]) + packed_gram(strips[...], scale)


def basis_body(sizes, evolved, sides, gram, basis, upper):
    vectors, layers, rows, columns = sizes
    groups = vectors // SUB
    shape = (SUB, columns)
    lane = lanes_of(shape)
    sub = lax.broadcasted_iota(jnp.int32, shape, 0)
    packed = gram[...]
    work = []
    for group in range(groups):
        turned = pltpu.roll(packed, (columns - group * vectors) % columns, 1)
        unit = jnp.where(lane - vectors == sub + group * SUB, 1.0, 0.0)
        work.append(jnp.where(lane < vectors, turned, unit))
    for home in range(groups):
        first = home * SUB
        column = {
            (group, j): jnp.broadcast_to(work[group][:, first + j : first + j + 1], shape)
            for group in range(home, groups)
            for j in range(SUB)
        }
        for at in range(SUB):
            inverse_pivot = jnp.broadcast_to((1.0 / column[home, at])[at : at + 1, :], shape)
            line = jnp.broadcast_to(work[home][at : at + 1, :], shape)
            for group in range(home, groups):
                factor = column[group, at] * inverse_pivot
                if group == home:
                    factor = jnp.where(sub > at, factor, 0.0)
                for j in range(at + 1, SUB):
                    level = jnp.broadcast_to(column[home, j][at : at + 1, :], shape)
                    if group == home:
                        column[home, j, "next"] = column[home, j] - factor * level
                    else:
                        column[group, j] = column[group, j] - factor * level
                work[group] = work[group] - factor * line
            for j in range(at + 1, SUB):
                column[home, j] = column.pop((home, j, "next"))
    inverse = []
    for group in range(groups):
        row = sub + group * SUB
        pivot = jnp.sum(jnp.where(lane == row, work[group], 0.0), axis=1, keepdims=True)
        done = work[group] * (1.0 / jnp.sqrt(jnp.broadcast_to(pivot, shape)))
        upper[pl.ds(group * SUB, SUB), :] = jnp.where(lane >= row, done, 0.0)[:, :vectors]
        inverse.append(pltpu.roll(done, columns - vectors, 1)[:, :vectors])
    inverse = jnp.concatenate(inverse, axis=0)
    stride = layers * rows
    at_edge = jnp.logical_or(lane < 2, lane >= columns - 2)
    wide = 2 if stride % 2 == 0 else 1

    def whole(at):
        layer, row = divmod(at, rows)
        parts = []
        for group in range(groups):
            edge = sides[pl.ds(layer * vectors + group * SUB, SUB), :]
            edge = pltpu.roll(edge, -(SPAN * (row + 2) + EDGE) % columns, 1)
            here = evolved[pl.ds(group * SUB, SUB), pl.ds(at * columns, columns)]
            parts.append(jnp.where(at_edge, edge, here))
        return jnp.concatenate(parts, axis=0)

    for first in range(0, stride, wide):
        part = jnp.dot(
            inverse, jnp.concatenate([whole(first + n) for n in range(wide)], axis=1),
            precision=lax.Precision.HIGHEST, preferred_element_type=jnp.float32,
        )
        for n in range(wide):
            for group in range(groups):
                at = pl.ds(group * SUB * stride + first + n, SUB, stride=stride)
                basis[at, :] = part[group * SUB : (group + 1) * SUB, n * columns : (n + 1) * columns]


def exchange(value, axis, partner):
    count = lax.axis_size(axis)
    return lax.ppermute(value, axis, [(i, partner(i)) for i in range(count)])


def local(base_stream, tangent_vectors):
    sizes = tangent_vectors.shape
    vectors, layers, rows, columns = sizes
    down, across = lax.axis_size("gy"), lax.axis_size("gx")
    assert layers == 2 and down & (down - 1) == 0 and across & (across - 1) == 0 and across > 1
    assert (rows + 4) * SPAN <= columns and columns >= 2 * SPAN and vectors * vectors == SUB * columns
    pv = tangent_vectors.reshape(vectors * layers * rows, columns)
    base = base_stream.reshape(layers * rows, columns)
    f32 = lambda *shape: jax.ShapeDtypeStruct(shape, jnp.float32)

    def call(body, outs, *operands, scratch=(), inputs=VMEM):
        return pl.pallas_call(
            lambda *refs: body(sizes, *refs),
            out_shape=outs,
            in_specs=[inputs] * len(operands),
            out_specs=[VMEM] * len(outs),
            scratch_shapes=scratch,
            compiler_params=pltpu.CompilerParams(vmem_limit_bytes=8 << 20),
        )(*operands)

    strip = f32(layers * 2 * vectors + SUB, columns)
    bottom, top = call(
        pack_rows_body, [strip, strip],
        pltpu.with_memory_space_constraint(tangent_vectors.reshape(vectors * layers, rows, columns), pltpu.HBM),
        pltpu.with_memory_space_constraint(base, pltpu.HBM),
        inputs=pl.BlockSpec(memory_space=pltpu.HBM),
        scratch=[
            pltpu.VMEM((vectors * layers, rows, columns), jnp.float32),
            pltpu.VMEM((layers * rows, columns), jnp.float32),
            pltpu.SemaphoreType.DMA((3,)),
        ],
    )
    above = exchange(bottom, "gy", lambda i: (i + 1) % down)
    below = exchange(top, "gy", lambda i: (i - 1) % down)
    cells = layers * rows * columns
    scale = 1.0 / (cells * down * across)
    parcel = f32(SUB + layers * (vectors + SUB), columns)
    evolved, message = call(
        lambda sizes, *refs: stencil_body(sizes, scale, *refs),
        [f32(vectors, cells), parcel],
        pv, base, above, below,
        scratch=[pltpu.VMEM((layers * rows, 4, SUB, columns), jnp.float32)],
    )
    half, sides = 1, ()
    while half < across:
        last = 2 * half == across
        got = exchange(message, "gx", lambda i: i ^ (2 * half - 1))
        body = lambda sizes, *refs, half=half, last=last: join_body(sizes, scale, half, last, *refs)
        message, *sides = call(
            body,
            [f32(SUB, columns) if last else parcel, f32(layers * vectors, columns)],
            message, got, *sides,
            scratch=[pltpu.VMEM((vectors, (2 if last else 1) * layers * columns), jnp.float32)],
        )
        half *= 2
    gram = message
    half = 1
    while half < down:
        gram = gram + exchange(gram, ("gy", "gx"), lambda i: ((i // across) ^ half) * across + ((i % across) ^ 1))
        half *= 2
    basis, upper = call(
        basis_body, [f32(vectors * layers * rows, columns), f32(vectors, vectors)], evolved, *sides, gram
    )
    return basis.reshape(sizes), upper


def solution(mesh):
    return jax.shard_map(
        local,
        mesh=mesh,
        in_specs=(P("ens", "gy", "gx"), P("ens", None, "gy", "gx")),
        out_specs=(P("ens", None, "gy", "gx"), P("ens", None)),
        check_vma=False,
    )
```

```python
import jax
import jax.numpy as jnp
from jax import lax
from jax.experimental import pallas as pl
from jax.experimental.pallas import tpu as pltpu
from jax.sharding import PartitionSpec as P

coupling_pair = (0.6, 0.3)
time_step = 0.05
hyper_visc = 0.1

SUB = 8
EDGE = 4
SPAN = 2 * EDGE
VMEM = pl.BlockSpec(memory_space=pltpu.VMEM)


def lanes_of(shape):
    return lax.broadcasted_iota(jnp.int32, shape, len(shape) - 1)


class Rows:
    def __init__(self, sizes, pv, base, above, below):
        self.vectors, self.layers, self.rows, self.columns = sizes
        self.groups = self.vectors // SUB
        self.pv, self.base, self.above, self.below = pv, base, above, below

    def halo(self, strip, layer, step, group):
        if group < self.groups:
            return strip[pl.ds((layer * 2 + step) * self.vectors + group * SUB, SUB), :]
        found = strip[pl.ds(self.layers * 2 * self.vectors + layer * 2 + step, 1), :]
        return jnp.broadcast_to(found, (SUB, self.columns))

    def own(self, layer, row, group):
        if group < self.groups:
            stride = self.layers * self.rows
            return self.pv[pl.ds(group * SUB * stride + layer * self.rows + row, SUB, stride=stride), :]
        return jnp.broadcast_to(self.base[pl.ds(layer * self.rows + row, 1), :], (SUB, self.columns))

    def get(self, layer, row, group):
        if row < 0:
            return self.halo(self.above, layer, row + 2, group)
        if row >= self.rows:
            return self.halo(self.below, layer, row - self.rows, group)
        return self.own(layer, row, group)


def pack_rows_body(sizes, pv, base, bottom, top, pv_rows, base_rows, done):
    vectors, layers, rows, columns = sizes
    ends = (0, rows - 2)
    copies = [
        pltpu.make_async_copy(pv.at[:, pl.ds(first, 2), :], pv_rows.at[:, pl.ds(first, 2), :], done.at[n])
        for n, first in enumerate(ends)
    ]
    copies.append(pltpu.make_async_copy(base, base_rows, done.at[2]))
    for copy in copies:
        copy.start()
    for copy in copies:
        copy.wait()
    source = Rows(sizes, pv_rows.reshape(vectors * layers * rows, columns), base_rows, None, None)
    for out, first in ((top, 0), (bottom, rows - 2)):
        for layer in range(layers):
            for step in range(2):
                for group in range(source.groups):
                    at = pl.ds((layer * 2 + step) * vectors + group * SUB, SUB)
                    out[at, :] = source.own(layer, first + step, group)
                at = pl.ds(layers * 2 * vectors + layer * 2 + step, 1)
                out[at, :] = source.own(layer, first + step, source.groups)[:1]
        out[pl.ds(layers * 2 * (vectors + 1), SUB - layers * 2), :] = jnp.zeros((SUB - layers * 2, columns), jnp.float32)


class Fields:
    pass


def base_weights(at, other, layer):
    c = coupling_pair[layer]
    a = 1.0 / (4.0 + c)
    j = 0.25 * time_step
    pv_dx = at.near_dx - (4.0 + c) * at.dx + c * other.dx
    pv_dy = at.near_dy - (4.0 + c) * at.dy + c * other.dy
    return (
        j * (at.dy + a * pv_dy),
        -j * (at.dx + a * pv_dx),
        (j * a * a) * pv_dy,
        (-j * a * a) * pv_dx,
    )


def stepped(at, other, layer, weights):
    c, c_other = coupling_pair[layer], coupling_pair[1 - layer]
    cross = c * (4.0 + c) / (4.0 + c_other)
    v = time_step * hyper_visc
    result = (1.0 - 20.0 * v) * at.value + (8.0 * v) * at.near - (2.0 * v) * at.diagonal - v * at.far
    result = result + (weights[0] * at.dx + weights[1] * at.dy)
    result = result + weights[2] * (at.near_dx + cross * other.dx)
    return result + weights[3] * (at.near_dy + cross * other.dy)


def gram_of(whole, scale):
    return lax.dot_general(
        whole, whole, (((1,), (1,)), ((), ())),
        precision=lax.Precision.HIGHEST, preferred_element_type=jnp.float32,
    ) * scale


def at_end(part, columns):
    return jnp.concatenate([jnp.zeros((SUB, columns - part.shape[1]), jnp.float32), part], axis=1)


def tile_fields(source, group, wanted, edge_rows, edges):
    layers, columns = source.layers, source.columns
    place = lanes_of((SUB, columns)) // SPAN
    value, dx, sx, dx2, sx2 = {}, {}, {}, {}, {}
    spread = sorted({row + n for row in wanted for n in range(-2, 3)} | set(edge_rows))
    beside = {row + n for row in wanted for n in range(-1, 2)}
    for layer in range(layers):
        packed = edges(layer, None)
        for row in spread:
            here = source.get(layer, row, group)
            value[layer, row] = here
            if row in edge_rows:
                turned = pltpu.roll(here, (EDGE + SPAN * (row + 2)) % columns, 1)
                packed = jnp.where(place == row + 2, turned, packed)
            if row in beside:
                west, east = pltpu.roll(here, 1, 1), pltpu.roll(here, columns - 1, 1)
                dx[layer, row], sx[layer, row] = east - west, east + west
            if row in wanted:
                west, east = pltpu.roll(here, 2, 1), pltpu.roll(here, columns - 2, 1)
                dx2[layer, row], sx2[layer, row] = east - west, east + west
        edges(layer, packed)
    found = {}
    for layer in range(layers):
        for row in wanted:
            up, down = (layer, row - 1), (layer, row + 1)
            at = found[layer, row] = Fields()
            at.value, at.dx = value[layer, row], dx[layer, row]
            at.dy = value[down] - value[up]
            at.near = sx[layer, row] + (value[down] + value[up])
            at.near_dx = dx2[layer, row] + (dx[down] + dx[up])
            at.near_dy = (sx[down] - sx[up]) + (value[layer, row + 2] - value[layer, row - 2])
            at.diagonal = sx[down] + sx[up]
            at.far = sx2[layer, row] + (value[layer, row + 2] + value[layer, row - 2])
    return found


def step_rows(source, wanted, edge_rows, edges_of, evolved, coef):
    lane = lanes_of((SUB, source.columns))
    inside = jnp.logical_and(lane >= 2, lane < source.columns - 2)
    order = [source.groups, *range(source.groups)]
    for group in order:
        found = tile_fields(source, group, wanted, edge_rows, edges_of(group))
        for layer in range(source.layers):
            for n, row in enumerate(wanted):
                at = layer * len(wanted) + n
                here, other = found[layer, row], found[1 - layer, row]
                if group == source.groups:
                    for w, weight in enumerate(base_weights(here, other, layer)):
                        coef[at, w] = weight
                    continue
                result = stepped(here, other, layer, [coef[at, w] for w in range(4)])
                block = pl.ds(group * SUB, SUB), pl.ds(at * source.columns, source.columns)
                evolved[block] = jnp.where(inside, result, 0.0)


def edge_place(sizes, layer, group):
    vectors, layers = sizes[:2]
    if group < vectors // SUB:
        return pl.ds(layer * vectors + group * SUB, SUB)
    return pl.ds(layers * vectors + layer, 1)


def row_sets(rows):
    return tuple(range(2, rows - 2)), (0, 1, rows - 2, rows - 1)


def middle_body(sizes, scale, pv, base, evolved, gram, edges, coef):
    vectors, layers, rows, columns = sizes
    source = Rows(sizes, pv, base, None, None)

    def edges_of(group):
        def put(layer, packed):
            if packed is None:
                return jnp.zeros((SUB, columns), jnp.float32)
            at = edge_place(sizes, layer, group)
            edges[at, :] = packed[: at.size]

        return put

    wanted, _ = row_sets(rows)
    step_rows(source, wanted, range(rows), edges_of, evolved, coef)
    edges[pl.ds(layers * (vectors + 1), SUB - layers), :] = jnp.zeros((SUB - layers, columns), jnp.float32)
    local = gram_of(evolved[...], scale)
    for at in range(0, vectors, SUB):
        gram[pl.ds(at, SUB), :] = at_end(local[at : at + SUB], columns)


def border_body(sizes, scale, pv, base, above, below, gram, edges, evolved, message, coef):
    vectors, layers, rows, columns = sizes
    source = Rows(sizes, pv, base, above, below)
    halo = (-2, -1, rows, rows + 1)

    def edges_of(group):
        def put(layer, packed):
            at = edge_place(sizes, layer, group)
            if packed is None:
                return jnp.broadcast_to(edges[at, :], (SUB, columns))
            message[at, :] = packed[: at.size]

        return put

    _, wanted = row_sets(rows)
    step_rows(source, wanted, halo, edges_of, evolved, coef)
    message[pl.ds(layers * (vectors + 1), SUB - layers), :] = jnp.zeros((SUB - layers, columns), jnp.float32)
    local = gram_of(evolved[...], scale)
    for at in range(0, vectors, SUB):
        message[pl.ds(at, SUB), :] = message[pl.ds(at, SUB), :] + (gram[pl.ds(at, SUB), :] + at_end(local[at : at + SUB], columns))


def strip_fields(here, columns):
    turn = lambda value, by: pltpu.roll(value, by % columns, 1)
    at = Fields()
    west, east = turn(here, 1), turn(here, -1)
    at.value, at.dx, sx = here, east - west, east + west
    west, east = turn(here, 2), turn(here, -2)
    dx2, sx2 = east - west, east + west
    up, down = turn(here, SPAN), turn(here, -SPAN)
    at.dy, at.near = down - up, sx + (down + up)
    at.near_dx = dx2 + (turn(at.dx, -SPAN) + turn(at.dx, SPAN))
    far_up, far_down = turn(here, 2 * SPAN), turn(here, -2 * SPAN)
    sx_up, sx_down = turn(sx, SPAN), turn(sx, -SPAN)
    at.near_dy = (sx_down - sx_up) + (far_down - far_up)
    at.diagonal, at.far = sx_down + sx_up, sx2 + (far_down + far_up)
    return at


def join_body(sizes, scale, half, last, *refs):
    vectors, layers, rows, columns = sizes
    refs = list(refs)
    mine, got = refs[:2]
    sides_in = refs[2] if half > 1 else None
    outs = refs[3:] if half > 1 else refs[2:]
    message, sides, strips = outs
    groups = vectors // SUB
    shape = (SUB, columns)
    lane = lanes_of(shape)
    column = lax.rem(lane, SPAN)
    west_half = column < EDGE
    valid = jnp.logical_and(
        jnp.logical_and(column >= 2, column < SPAN - 2),
        jnp.logical_and(lane >= 2 * SPAN, lane < (rows + 2) * SPAN),
    )
    tile = lax.axis_index("gx")
    spot = lax.rem(tile, 2 * half)
    first = spot < half
    mid_mine = jnp.logical_xor(west_half, jnp.logical_not(first))
    keep_mid = jnp.logical_or(jnp.logical_and(west_half, spot == half - 1), jnp.logical_and(~west_half, spot == half))
    keep_wrap = jnp.logical_or(jnp.logical_and(west_half, spot == 2 * half - 1), jnp.logical_and(~west_half, spot == 0))
    kinds = (False, True) if last else (False,)
    weights = {}
    parcel = {}
    for group in (groups, *range(groups)):
        found = {}
        for layer in range(layers):
            at = edge_place(sizes, layer, group)
            here, there = mine[at, :], got[at, :]
            if group < groups and layer == 0:
                parcel[group] = here + there
            here, there = jnp.broadcast_to(here, shape), jnp.broadcast_to(there, shape)
            mid, outer = jnp.where(mid_mine, here, there), jnp.where(mid_mine, there, here)
            if not last:
                message[at, :] = outer[: at.size]
            found[layer, False] = strip_fields(mid, columns)
            if last:
                found[layer, True] = strip_fields(outer, columns)
        for layer in range(layers):
            own = None
            for wrap in kinds:
                at, other = found[layer, wrap], found[1 - layer, wrap]
                if group == groups:
                    weights[layer, wrap] = base_weights(at, other, layer)
                    continue
                result = jnp.where(valid, stepped(at, other, layer, weights[layer, wrap]), 0.0)
                strips[pl.ds(group * SUB, SUB), pl.ds((layer * len(kinds) + wrap) * columns, columns)] = result
                where = pl.ds(layer * vectors + group * SUB, SUB)
                if own is None:
                    own = sides_in[where, :] if half > 1 else jnp.zeros(shape, jnp.float32)
                own = jnp.where(keep_wrap if wrap else keep_mid, result, own)
                if wrap == last:
                    sides[where, :] = own
    if not last:
        message[pl.ds(layers * (vectors + 1), SUB - layers), :] = jnp.zeros((SUB - layers, columns), jnp.float32)
    local = gram_of(strips[...], scale)
    total = jnp.zeros(shape, jnp.float32)
    free = columns - vectors
    for group in range(groups):
        block = pl.ds(group * SUB, SUB)
        joined = parcel[group] + at_end(local[group * SUB : (group + 1) * SUB], columns)
        if last:
            turned = pltpu.roll(joined, (vectors * (group + 1)) % columns, 1) if group + 1 < groups else joined
            total = jnp.where(lane // vectors == group, turned, total)
        else:
            message[block, :] = jnp.where(lane >= free, joined, message[block, :])
    if last:
        message[...] = total


def ready_body(sizes, middle, border, sides, parts):
    vectors, layers, rows, columns = sizes
    lane = lanes_of((SUB * 2, columns))
    at_edge = jnp.logical_or(lane < 2, lane >= columns - 2)
    sets = row_sets(rows)
    pair = 2 * SUB
    for layer in range(layers):
        for row in range(rows):
            which = 0 if row in sets[0] else 1
            block = layer * len(sets[which]) + sets[which].index(row)
            for first in range(0, vectors, pair):
                edge = sides[pl.ds(layer * vectors + first, pair), :]
                edge = pltpu.roll(edge, -(SPAN * (row + 2) + EDGE) % columns, 1)
                here = (middle, border)[which][pl.ds(first, pair), pl.ds(block * columns, columns)]
                rest = jnp.where(at_edge, edge, here)
                for n in range(3):
                    part = rest.astype(jnp.bfloat16)
                    if n < 2:
                        rest = rest - part.astype(jnp.float32)
                    parts[pl.ds(n * vectors + first, pair), pl.ds((layer * rows + row) * columns, columns)] = part


def basis_body(sizes, parts, gram, basis, upper):
    vectors, layers, rows, columns = sizes
    groups = vectors // SUB
    shape = (SUB, columns)
    lane = lanes_of(shape)
    sub = lax.broadcasted_iota(jnp.int32, shape, 0)
    packed = gram[...]
    work = []
    for group in range(groups):
        turned = pltpu.roll(packed, (columns - group * vectors) % columns, 1)
        unit = jnp.where(lane - vectors == sub + group * SUB, 1.0, 0.0)
        work.append(jnp.where(lane < vectors, turned, unit))
    for home in range(groups):
        first = home * SUB
        column = {
            (group, j): jnp.broadcast_to(work[group][:, first + j : first + j + 1], shape)
            for group in range(home, groups)
            for j in range(SUB)
        }
        for at in range(SUB):
            inverse_pivot = jnp.broadcast_to((1.0 / column[home, at])[at : at + 1, :], shape)
            line = jnp.broadcast_to(work[home][at : at + 1, :], shape)
            for group in range(home, groups):
                factor = column[group, at] * inverse_pivot
                if group == home:
                    factor = jnp.where(sub > at, factor, 0.0)
                for j in range(at + 1, SUB):
                    level = jnp.broadcast_to(column[home, j][at : at + 1, :], shape)
                    if group == home:
                        column[home, j, "next"] = column[home, j] - factor * level
                    else:
                        column[group, j] = column[group, j] - factor * level
                work[group] = work[group] - factor * line
            for j in range(at + 1, SUB):
                column[home, j] = column.pop((home, j, "next"))
    order = ((0, 0), (1, 0), (2, 0), (0, 1), (1, 1), (0, 2))
    slot = lane // vectors
    inverse = []
    for group in range(groups):
        row = sub + group * SUB
        pivot = jnp.sum(jnp.where(lane == row, work[group], 0.0), axis=1, keepdims=True)
        done = work[group] * (1.0 / jnp.sqrt(jnp.broadcast_to(pivot, shape)))
        upper[pl.ds(group * SUB, SUB), :] = jnp.where(lane >= row, done, 0.0)[:, :vectors]
        rest, terms = jnp.where(slot == 1, done, 0.0), []
        for _ in range(3):
            term = rest.astype(jnp.bfloat16).astype(jnp.float32)
            rest = rest - term
            terms.append(term)
        per = columns // vectors
        wide = []
        for first in range(0, len(order), per):
            line = jnp.zeros(shape, jnp.float32)
            for n, (mine, _) in enumerate(order[first : first + per]):
                line = line + pltpu.roll(terms[mine], (n - 1) * vectors % columns, 1)
            wide.append(line)
        inverse.append(jnp.concatenate(wide, axis=1))
    inverse = jnp.concatenate(inverse, axis=0).astype(jnp.bfloat16)[:, : len(order) * vectors]
    stride = layers * rows
    wide = 2 if stride % 2 == 0 else 1
    for first in range(0, stride, wide):
        at = pl.ds(first * columns, wide * columns)
        split = [parts[pl.ds(n * vectors, vectors), at] for n in range(3)]
        part = jnp.dot(
            inverse, jnp.concatenate([split[n] for _, n in order], axis=0), preferred_element_type=jnp.float32
        )
        for n in range(wide):
            for group in range(groups):
                at = pl.ds(group * SUB * stride + first + n, SUB, stride=stride)
                basis[at, :] = part[group * SUB : (group + 1) * SUB, n * columns : (n + 1) * columns]


def exchange(value, axis, partner):
    count = lax.axis_size(axis)
    return lax.ppermute(value, axis, [(i, partner(i)) for i in range(count)])


def local(base_stream, tangent_vectors):
    sizes = tangent_vectors.shape
    vectors, layers, rows, columns = sizes
    down, across = lax.axis_size("gy"), lax.axis_size("gx")
    assert layers == 2 and down & (down - 1) == 0 and across & (across - 1) == 0 and across > 1
    assert rows >= 5 and (rows + 4) * SPAN + vectors <= columns and vectors * vectors == SUB * columns
    assert vectors % (2 * SUB) == 0
    pv = tangent_vectors.reshape(vectors * layers * rows, columns)
    base = base_stream.reshape(layers * rows, columns)
    f32 = lambda *shape: jax.ShapeDtypeStruct(shape, jnp.float32)

    def call(body, outs, *operands, scratch=(), inputs=VMEM):
        return pl.pallas_call(
            lambda *refs: body(sizes, *refs),
            out_shape=outs,
            in_specs=[inputs] * len(operands),
            out_specs=[VMEM] * len(outs),
            scratch_shapes=scratch,
            compiler_params=pltpu.CompilerParams(vmem_limit_bytes=8 << 20),
        )(*operands)

    strip = f32(layers * 2 * vectors + SUB, columns)
    bottom, top = call(
        pack_rows_body, [strip, strip],
        pltpu.with_memory_space_constraint(tangent_vectors.reshape(vectors * layers, rows, columns), pltpu.HBM),
        pltpu.with_memory_space_constraint(base, pltpu.HBM),
        inputs=pl.BlockSpec(memory_space=pltpu.HBM),
        scratch=[
            pltpu.VMEM((vectors * layers, rows, columns), jnp.float32),
            pltpu.VMEM((layers * rows, columns), jnp.float32),
            pltpu.SemaphoreType.DMA((3,)),
        ],
    )
    above = exchange(bottom, "gy", lambda i: (i + 1) % down)
    below = exchange(top, "gy", lambda i: (i - 1) % down)
    cells = layers * rows * columns
    scale = 1.0 / (cells * down * across)
    parcel = f32(layers * vectors + SUB, columns)
    middle_rows, border_rows = (layers * len(part) for part in row_sets(rows))
    middle, gram, edges = call(
        lambda sizes, *refs: middle_body(sizes, scale, *refs),
        [f32(vectors, middle_rows * columns), f32(vectors, columns), parcel],
        pv, base,
        scratch=[pltpu.VMEM((middle_rows, 4, SUB, columns), jnp.float32)],
    )
    border, message = call(
        lambda sizes, *refs: border_body(sizes, scale, *refs),
        [f32(vectors, border_rows * columns), parcel],
        pv, base, above, below, gram, edges,
        scratch=[pltpu.VMEM((border_rows, 4, SUB, columns), jnp.float32)],
    )
    half, sides = 1, ()
    while half < across:
        last = 2 * half == across
        got = exchange(message, "gx", lambda i: i ^ (2 * half - 1))
        body = lambda sizes, *refs, half=half, last=last: join_body(sizes, scale, half, last, *refs)
        message, *sides = call(
            body,
            [f32(SUB, columns) if last else parcel, f32(layers * vectors, columns)],
            message, got, *sides,
            scratch=[pltpu.VMEM((vectors, (2 if last else 1) * layers * columns), jnp.float32)],
        )
        half *= 2
    (parts,) = call(ready_body, [jax.ShapeDtypeStruct((3 * vectors, cells), jnp.bfloat16)], middle, border, *sides)
    gram = message
    half = 1
    while half < down:
        got = exchange(gram, ("gy", "gx"), lambda i: ((i // across) ^ half) * across + ((i % across) ^ 1))
        gram = gram + got
        half *= 2
    basis, upper = call(
        basis_body, [f32(vectors * layers * rows, columns), f32(vectors, vectors)], parts, gram
    )
    return basis.reshape(sizes), upper


def solution(mesh):
    return jax.shard_map(
        local,
        mesh=mesh,
        in_specs=(P("ens", "gy", "gx"), P("ens", None, "gy", "gx")),
        out_specs=(P("ens", None, "gy", "gx"), P("ens", None)),
        check_vma=False,
    )
```

```python
import jax
import jax.numpy as jnp
from jax import lax
from jax.experimental import pallas as pl
from jax.experimental.pallas import tpu as pltpu
from jax.sharding import PartitionSpec as P

coupling_pair = (0.6, 0.3)
time_step = 0.05
hyper_visc = 0.1

SUB = 8
EDGE = 4
SPAN = 2 * EDGE
VMEM = pl.BlockSpec(memory_space=pltpu.VMEM)


def lanes_of(shape):
    return lax.broadcasted_iota(jnp.int32, shape, len(shape) - 1)


class Rows:
    def __init__(self, sizes, pv, base, above, below):
        self.vectors, self.layers, self.rows, self.columns = sizes
        self.groups = self.vectors // SUB
        self.pv, self.base, self.above, self.below = pv, base, above, below

    def halo(self, strip, layer, step, group):
        if group < self.groups:
            return strip[pl.ds((layer * 2 + step) * self.vectors + group * SUB, SUB), :]
        found = strip[pl.ds(self.layers * 2 * self.vectors + layer * 2 + step, 1), :]
        return jnp.broadcast_to(found, (SUB, self.columns))

    def own(self, layer, row, group):
        if group < self.groups:
            stride = self.layers * self.rows
            return self.pv[pl.ds(group * SUB * stride + layer * self.rows + row, SUB, stride=stride), :]
        return jnp.broadcast_to(self.base[pl.ds(layer * self.rows + row, 1), :], (SUB, self.columns))

    def get(self, layer, row, group):
        if row < 0:
            return self.halo(self.above, layer, row + 2, group)
        if row >= self.rows:
            return self.halo(self.below, layer, row - self.rows, group)
        return self.own(layer, row, group)


def pack_rows_body(sizes, pv, base, bottom, top, pv_rows, base_rows, done):
    vectors, layers, rows, columns = sizes
    ends = (0, rows - 2)
    copies = [
        pltpu.make_async_copy(pv.at[:, pl.ds(first, 2), :], pv_rows.at[:, pl.ds(first, 2), :], done.at[n])
        for n, first in enumerate(ends)
    ]
    copies.append(pltpu.make_async_copy(base, base_rows, done.at[2]))
    for copy in copies:
        copy.start()
    for copy in copies:
        copy.wait()
    source = Rows(sizes, pv_rows.reshape(vectors * layers * rows, columns), base_rows, None, None)
    for out, first in ((top, 0), (bottom, rows - 2)):
        for layer in range(layers):
            for step in range(2):
                for group in range(source.groups):
                    at = pl.ds((layer * 2 + step) * vectors + group * SUB, SUB)
                    out[at, :] = source.own(layer, first + step, group)
                at = pl.ds(layers * 2 * vectors + layer * 2 + step, 1)
                out[at, :] = source.own(layer, first + step, source.groups)[:1]
        out[pl.ds(layers * 2 * (vectors + 1), SUB - layers * 2), :] = jnp.zeros((SUB - layers * 2, columns), jnp.float32)


class Fields:
    pass


def base_weights(at, other, layer):
    c = coupling_pair[layer]
    a = 1.0 / (4.0 + c)
    j = 0.25 * time_step
    pv_dx = at.near_dx - (4.0 + c) * at.dx + c * other.dx
    pv_dy = at.near_dy - (4.0 + c) * at.dy + c * other.dy
    return (
        j * (at.dy + a * pv_dy),
        -j * (at.dx + a * pv_dx),
        (j * a * a) * pv_dy,
        (-j * a * a) * pv_dx,
    )


def stepped(at, other, layer, weights):
    c, c_other = coupling_pair[layer], coupling_pair[1 - layer]
    cross = c * (4.0 + c) / (4.0 + c_other)
    v = time_step * hyper_visc
    result = (1.0 - 20.0 * v) * at.value + (8.0 * v) * at.near - (2.0 * v) * at.diagonal - v * at.far
    result = result + (weights[0] * at.dx + weights[1] * at.dy)
    result = result + weights[2] * (at.near_dx + cross * other.dx)
    return result + weights[3] * (at.near_dy + cross * other.dy)


def gram_of(whole, scale):
    return lax.dot_general(
        whole, whole, (((1,), (1,)), ((), ())),
        precision=lax.Precision.HIGHEST, preferred_element_type=jnp.float32,
    ) * scale


def at_end(part, columns):
    return jnp.concatenate([jnp.zeros((SUB, columns - part.shape[1]), jnp.float32), part], axis=1)


def tile_fields(source, group, wanted, edge_rows, edges):
    layers, columns = source.layers, source.columns
    place = lanes_of((SUB, columns)) // SPAN
    value, dx, sx, dx2, sx2 = {}, {}, {}, {}, {}
    spread = sorted({row + n for row in wanted for n in range(-2, 3)} | set(edge_rows))
    beside = {row + n for row in wanted for n in range(-1, 2)}
    for layer in range(layers):
        packed = edges(layer, None)
        for row in spread:
            here = source.get(layer, row, group)
            value[layer, row] = here
            if row in edge_rows:
                turned = pltpu.roll(here, (EDGE + SPAN * (row + 2)) % columns, 1)
                packed = jnp.where(place == row + 2, turned, packed)
            if row in beside:
                west, east = pltpu.roll(here, 1, 1), pltpu.roll(here, columns - 1, 1)
                dx[layer, row], sx[layer, row] = east - west, east + west
            if row in wanted:
                west, east = pltpu.roll(here, 2, 1), pltpu.roll(here, columns - 2, 1)
                dx2[layer, row], sx2[layer, row] = east - west, east + west
        edges(layer, packed)
    found = {}
    for layer in range(layers):
        for row in wanted:
            up, down = (layer, row - 1), (layer, row + 1)
            at = found[layer, row] = Fields()
            at.value, at.dx = value[layer, row], dx[layer, row]
            at.dy = value[down] - value[up]
            at.near = sx[layer, row] + (value[down] + value[up])
            at.near_dx = dx2[layer, row] + (dx[down] + dx[up])
            at.near_dy = (sx[down] - sx[up]) + (value[layer, row + 2] - value[layer, row - 2])
            at.diagonal = sx[down] + sx[up]
            at.far = sx2[layer, row] + (value[layer, row + 2] + value[layer, row - 2])
    return found


def step_rows(source, wanted, edge_rows, edges_of, evolved, coef):
    lane = lanes_of((SUB, source.columns))
    inside = jnp.logical_and(lane >= 2, lane < source.columns - 2)
    order = [source.groups, *range(source.groups)]
    for group in order:
        found = tile_fields(source, group, wanted, edge_rows, edges_of(group))
        for layer in range(source.layers):
            for n, row in enumerate(wanted):
                at = layer * len(wanted) + n
                here, other = found[layer, row], found[1 - layer, row]
                if group == source.groups:
                    for w, weight in enumerate(base_weights(here, other, layer)):
                        coef[at, w] = weight
                    continue
                result = stepped(here, other, layer, [coef[at, w] for w in range(4)])
                block = pl.ds(group * SUB, SUB), pl.ds(at * source.columns, source.columns)
                evolved[block] = jnp.where(inside, result, 0.0)


def edge_place(sizes, layer, group):
    vectors, layers = sizes[:2]
    if group < vectors // SUB:
        return pl.ds(layer * vectors + group * SUB, SUB)
    return pl.ds(layers * vectors + layer, 1)


def row_sets(rows):
    return tuple(range(2, rows - 2)), (0, 1), (rows - 2, rows - 1)


def rows_body(sizes, scale, wanted, edge_rows, below_only, pv, base, *refs):
    vectors, layers, _, columns = sizes
    refs = list(refs)
    halo = refs.pop(0) if below_only is not None else None
    before = [refs.pop(0), refs.pop(0)] if below_only is not None else None
    evolved, gram, edges, coef = refs if below_only is not True else (refs[0], None, refs[1], refs[2])
    source = Rows(sizes, pv, base, halo, halo)

    def edges_of(group):
        def put(layer, packed):
            at = edge_place(sizes, layer, group)
            if packed is not None:
                edges[at, :] = packed[: at.size]
            elif before is None:
                return jnp.zeros((SUB, columns), jnp.float32)
            else:
                return jnp.broadcast_to(before[1][at, :], (SUB, columns))

        return put

    step_rows(source, wanted, edge_rows, edges_of, evolved, coef)
    edges[pl.ds(layers * (vectors + 1), SUB - layers), :] = jnp.zeros((SUB - layers, columns), jnp.float32)
    local = gram_of(evolved[...], scale)
    for first in range(0, vectors, SUB):
        at = pl.ds(first, SUB)
        total = at_end(local[first : first + SUB], columns)
        if before is not None:
            total = before[0][at, :] + total
        if gram is not None:
            gram[at, :] = total
        else:
            edges[at, :] = edges[at, :] + total


def strip_fields(here, columns):
    turn = lambda value, by: pltpu.roll(value, by % columns, 1)
    at = Fields()
    west, east = turn(here, 1), turn(here, -1)
    at.value, at.dx, sx = here, east - west, east + west
    west, east = turn(here, 2), turn(here, -2)
    dx2, sx2 = east - west, east + west
    up, down = turn(here, SPAN), turn(here, -SPAN)
    at.dy, at.near = down - up, sx + (down + up)
    at.near_dx = dx2 + (turn(at.dx, -SPAN) + turn(at.dx, SPAN))
    far_up, far_down = turn(here, 2 * SPAN), turn(here, -2 * SPAN)
    sx_up, sx_down = turn(sx, SPAN), turn(sx, -SPAN)
    at.near_dy = (sx_down - sx_up) + (far_down - far_up)
    at.diagonal, at.far = sx_down + sx_up, sx2 + (far_down + far_up)
    return at


def join_body(sizes, scale, half, last, *refs):
    vectors, layers, rows, columns = sizes
    refs = list(refs)
    mine, got = refs[:2]
    sides_in = refs[2] if half > 1 else None
    outs = refs[3:] if half > 1 else refs[2:]
    message, sides, strips = outs
    groups = vectors // SUB
    shape = (SUB, columns)
    lane = lanes_of(shape)
    column = lax.rem(lane, SPAN)
    west_half = column < EDGE
    valid = jnp.logical_and(
        jnp.logical_and(column >= 2, column < SPAN - 2),
        jnp.logical_and(lane >= 2 * SPAN, lane < (rows + 2) * SPAN),
    )
    tile = lax.axis_index("gx")
    spot = lax.rem(tile, 2 * half)
    first = spot < half
    mid_mine = jnp.logical_xor(west_half, jnp.logical_not(first))
    keep_mid = jnp.logical_or(jnp.logical_and(west_half, spot == half - 1), jnp.logical_and(~west_half, spot == half))
    keep_wrap = jnp.logical_or(jnp.logical_and(west_half, spot == 2 * half - 1), jnp.logical_and(~west_half, spot == 0))
    kinds = (False, True) if last else (False,)
    weights = {}
    parcel = {}
    for group in (groups, *range(groups)):
        found = {}
        for layer in range(layers):
            at = edge_place(sizes, layer, group)
            here, there = mine[at, :], got[at, :]
            if group < groups and layer == 0:
                parcel[group] = here + there
            here, there = jnp.broadcast_to(here, shape), jnp.broadcast_to(there, shape)
            mid, outer = jnp.where(mid_mine, here, there), jnp.where(mid_mine, there, here)
            if not last:
                message[at, :] = outer[: at.size]
            found[layer, False] = strip_fields(mid, columns)
            if last:
                found[layer, True] = strip_fields(outer, columns)
        for layer in range(layers):
            own = None
            for wrap in kinds:
                at, other = found[layer, wrap], found[1 - layer, wrap]
                if group == groups:
                    weights[layer, wrap] = base_weights(at, other, layer)
                    continue
                result = jnp.where(valid, stepped(at, other, layer, weights[layer, wrap]), 0.0)
                strips[pl.ds(group * SUB, SUB), pl.ds((layer * len(kinds) + wrap) * columns, columns)] = result
                where = pl.ds(layer * vectors + group * SUB, SUB)
                if own is None:
                    own = sides_in[where, :] if half > 1 else jnp.zeros(shape, jnp.float32)
                own = jnp.where(keep_wrap if wrap else keep_mid, result, own)
                if wrap == last:
                    sides[where, :] = own
    if not last:
        message[pl.ds(layers * (vectors + 1), SUB - layers), :] = jnp.zeros((SUB - layers, columns), jnp.float32)
    local = gram_of(strips[...], scale)
    total = jnp.zeros(shape, jnp.float32)
    free = columns - vectors
    for group in range(groups):
        block = pl.ds(group * SUB, SUB)
        joined = parcel[group] + at_end(local[group * SUB : (group + 1) * SUB], columns)
        if last:
            turned = pltpu.roll(joined, (vectors * (group + 1)) % columns, 1) if group + 1 < groups else joined
            total = jnp.where(lane // vectors == group, turned, total)
        else:
            message[block, :] = jnp.where(lane >= free, joined, message[block, :])
    if last:
        message[...] = total


def ready_body(sizes, middle, upper_rows, lower_rows, sides, parts):
    vectors, layers, rows, columns = sizes
    lane = lanes_of((SUB * 2, columns))
    at_edge = jnp.logical_or(lane < 2, lane >= columns - 2)
    sets = row_sets(rows)
    pair = 2 * SUB
    for layer in range(layers):
        for row in range(rows):
            which = [row in part for part in sets].index(True)
            block = layer * len(sets[which]) + sets[which].index(row)
            for first in range(0, vectors, pair):
                edge = sides[pl.ds(layer * vectors + first, pair), :]
                edge = pltpu.roll(edge, -(SPAN * (row + 2) + EDGE) % columns, 1)
                here = (middle, upper_rows, lower_rows)[which][pl.ds(first, pair), pl.ds(block * columns, columns)]
                rest = jnp.where(at_edge, edge, here)
                for n in range(3):
                    part = rest.astype(jnp.bfloat16)
                    if n < 2:
                        rest = rest - part.astype(jnp.float32)
                    parts[pl.ds(n * vectors + first, pair), pl.ds((layer * rows + row) * columns, columns)] = part


def basis_body(sizes, parts, gram, basis, upper):
    vectors, layers, rows, columns = sizes
    groups = vectors // SUB
    shape = (SUB, columns)
    lane = lanes_of(shape)
    sub = lax.broadcasted_iota(jnp.int32, shape, 0)
    packed = gram[...]
    work = []
    for group in range(groups):
        turned = pltpu.roll(packed, (columns - group * vectors) % columns, 1)
        unit = jnp.where(lane - vectors == sub + group * SUB, 1.0, 0.0)
        work.append(jnp.where(lane < vectors, turned, unit))
    order = ((0, 0), (1, 0), (2, 0), (0, 1), (1, 1), (0, 2))
    per = columns // vectors
    inverse = []
    for home in range(groups):
        first = home * SUB
        column = {
            (group, j): jnp.broadcast_to(work[group][:, first + j : first + j + 1], shape)
            for group in range(home, groups)
            for j in range(SUB)
        }
        root = jnp.ones(shape, jnp.float32)
        for at in range(SUB):
            inverse_pivot = jnp.broadcast_to((1.0 / column[home, at])[at : at + 1, :], shape)
            line = jnp.broadcast_to(work[home][at : at + 1, :], shape)
            root = jnp.where(sub == at, column[home, at], root)
            for group in range(home, groups):
                factor = column[group, at] * inverse_pivot
                if group == home:
                    factor = jnp.where(sub > at, factor, 0.0)
                for j in range(at + 1, SUB):
                    level = jnp.broadcast_to(column[home, j][at : at + 1, :], shape)
                    if group == home:
                        column[home, j, "next"] = column[home, j] - factor * level
                    else:
                        column[group, j] = column[group, j] - factor * level
                work[group] = work[group] - factor * line
            for j in range(at + 1, SUB):
                column[home, j] = column.pop((home, j, "next"))
        scaled = work[home] * (1.0 / jnp.sqrt(root))
        upper[pl.ds(home * SUB, SUB), :] = jnp.where(lane >= sub + home * SUB, scaled, 0.0)[:, :vectors]
        rest, terms = jnp.where(lane // vectors == 1, scaled, 0.0), []
        for _ in range(3):
            term = rest.astype(jnp.bfloat16).astype(jnp.float32)
            rest = rest - term
            terms.append(term)
        wide = []
        for first in range(0, len(order), per):
            line = jnp.zeros(shape, jnp.float32)
            for n, (mine, _) in enumerate(order[first : first + per]):
                line = line + pltpu.roll(terms[mine], (n - 1) * vectors % columns, 1)
            wide.append(line)
        inverse.append(jnp.concatenate(wide, axis=1))
    inverse = jnp.concatenate(inverse, axis=0).astype(jnp.bfloat16)[:, : len(order) * vectors]
    wide = 2 if rows % 2 == 0 else 1
    flat = basis
    stride = layers * rows
    for first in range(0, stride, wide):
        at = pl.ds(first * columns, wide * columns)
        split = [parts[pl.ds(n * vectors, vectors), at] for n in range(3)]
        part = jnp.dot(
            inverse, jnp.concatenate([split[n] for _, n in order], axis=0), preferred_element_type=jnp.float32
        )
        for n in range(wide):
            for group in range(groups):
                at = pl.ds(group * SUB * stride + first + n, SUB, stride=stride)
                flat[at, :] = part[group * SUB : (group + 1) * SUB, n * columns : (n + 1) * columns]


def exchange(value, axis, partner):
    count = lax.axis_size(axis)
    return lax.ppermute(value, axis, [(i, partner(i)) for i in range(count)])


def local(base_stream, tangent_vectors):
    sizes = tangent_vectors.shape
    vectors, layers, rows, columns = sizes
    down, across = lax.axis_size("gy"), lax.axis_size("gx")
    assert layers == 2 and down & (down - 1) == 0 and across & (across - 1) == 0 and across > 1
    assert rows >= 5 and (rows + 4) * SPAN + vectors <= columns and vectors * vectors == SUB * columns
    assert vectors % (2 * SUB) == 0
    pv = tangent_vectors.reshape(vectors * layers * rows, columns)
    base = base_stream.reshape(layers * rows, columns)
    f32 = lambda *shape: jax.ShapeDtypeStruct(shape, jnp.float32)

    def call(body, outs, *operands, scratch=(), inputs=VMEM, first_out=VMEM):
        return pl.pallas_call(
            lambda *refs: body(sizes, *refs),
            out_shape=outs,
            in_specs=[inputs] * len(operands),
            out_specs=[first_out] + [VMEM] * (len(outs) - 1),
            scratch_shapes=scratch,
            compiler_params=pltpu.CompilerParams(vmem_limit_bytes=8 << 20),
        )(*operands)

    strip = f32(layers * 2 * vectors + SUB, columns)
    bottom, top = call(
        pack_rows_body, [strip, strip],
        pltpu.with_memory_space_constraint(tangent_vectors.reshape(vectors * layers, rows, columns), pltpu.HBM),
        pltpu.with_memory_space_constraint(base, pltpu.HBM),
        inputs=pl.BlockSpec(memory_space=pltpu.HBM),
        scratch=[
            pltpu.VMEM((vectors * layers, rows, columns), jnp.float32),
            pltpu.VMEM((layers * rows, columns), jnp.float32),
            pltpu.SemaphoreType.DMA((3,)),
        ],
    )
    above = exchange(bottom, "gy", lambda i: (i + 1) % down)
    below = exchange(top, "gy", lambda i: (i - 1) % down)
    cells = layers * rows * columns
    scale = 1.0 / (cells * down * across)
    parcel = f32(layers * vectors + SUB, columns)
    middle_set, upper_set, lower_set = row_sets(rows)

    def rows_call(wanted, edge_rows, below_only, *operands):
        blocks = layers * len(wanted)
        return call(
            lambda sizes, *refs: rows_body(sizes, scale, wanted, edge_rows, below_only, *refs),
            [f32(vectors, blocks * columns)] + [f32(vectors, columns)] * (below_only is not True) + [parcel],
            pv, base, *operands,
            scratch=[pltpu.VMEM((blocks, 4, SUB, columns), jnp.float32)],
        )

    middle, gram, edges = rows_call(middle_set, range(rows), None)
    upper_rows, gram, edges = rows_call(upper_set, (-2, -1), False, above, gram, edges)
    lower_rows, message = rows_call(lower_set, (rows, rows + 1), True, below, gram, edges)
    half, sides = 1, ()
    while half < across:
        last = 2 * half == across
        got = exchange(message, "gx", lambda i: i ^ (2 * half - 1))
        body = lambda sizes, *refs, half=half, last=last: join_body(sizes, scale, half, last, *refs)
        message, *sides = call(
            body,
            [f32(SUB, columns) if last else parcel, f32(layers * vectors, columns)],
            message, got, *sides,
            scratch=[pltpu.VMEM((vectors, (2 if last else 1) * layers * columns), jnp.float32)],
        )
        half *= 2
    (parts,) = call(ready_body, [jax.ShapeDtypeStruct((3 * vectors, cells), jnp.bfloat16)], middle, upper_rows, lower_rows, *sides)
    gram = message
    half = 1
    while half < down:
        got = exchange(gram, ("gy", "gx"), lambda i: ((i // across) ^ half) * across + ((i % across) ^ 1))
        gram = gram + got
        half *= 2
    basis, upper = call(
        basis_body, [f32(vectors * layers * rows, columns), f32(vectors, vectors)], parts, gram
    )
    return basis.reshape(sizes), upper


def solution(mesh):
    return jax.shard_map(
        local,
        mesh=mesh,
        in_specs=(P("ens", "gy", "gx"), P("ens", None, "gy", "gx")),
        out_specs=(P("ens", None, "gy", "gx"), P("ens", None)),
        check_vma=False,
    )
```

```python
import jax
import jax.numpy as jnp
from jax import lax
from jax.experimental import pallas as pl
from jax.experimental.pallas import tpu as pltpu
from jax.sharding import PartitionSpec as P

coupling_pair = (0.6, 0.3)
time_step = 0.05
hyper_visc = 0.1

SUB = 8
EDGE = 4
SPAN = 2 * EDGE
VMEM = pl.BlockSpec(memory_space=pltpu.VMEM)


def lanes_of(shape):
    return lax.broadcasted_iota(jnp.int32, shape, len(shape) - 1)


class Rows:
    def __init__(self, sizes, pv, base, above, below):
        self.vectors, self.layers, self.rows, self.columns = sizes
        self.groups = self.vectors // SUB
        self.pv, self.base, self.above, self.below = pv, base, above, below

    def halo(self, strip, layer, step, group):
        if group < self.groups:
            return strip[pl.ds((layer * 2 + step) * self.vectors + group * SUB, SUB), :]
        found = strip[pl.ds(self.layers * 2 * self.vectors + layer * 2 + step, 1), :]
        return jnp.broadcast_to(found, (SUB, self.columns))

    def own(self, layer, row, group):
        if group < self.groups:
            stride = self.layers * self.rows
            return self.pv[pl.ds(group * SUB * stride + layer * self.rows + row, SUB, stride=stride), :]
        return jnp.broadcast_to(self.base[pl.ds(layer * self.rows + row, 1), :], (SUB, self.columns))

    def get(self, layer, row, group):
        if row < 0:
            return self.halo(self.above, layer, row + 2, group)
        if row >= self.rows:
            return self.halo(self.below, layer, row - self.rows, group)
        return self.own(layer, row, group)


def pack_rows_body(sizes, pv, base, bottom, top, pv_rows, base_rows, done):
    vectors, layers, rows, columns = sizes
    ends = (0, rows - 2)
    copies = [
        pltpu.make_async_copy(pv.at[:, pl.ds(first, 2), :], pv_rows.at[:, pl.ds(first, 2), :], done.at[n])
        for n, first in enumerate(ends)
    ]
    copies.append(pltpu.make_async_copy(base, base_rows, done.at[2]))
    for copy in copies:
        copy.start()
    for copy in copies:
        copy.wait()
    source = Rows(sizes, pv_rows.reshape(vectors * layers * rows, columns), base_rows, None, None)
    for out, first in ((top, 0), (bottom, rows - 2)):
        for layer in range(layers):
            for step in range(2):
                for group in range(source.groups):
                    at = pl.ds((layer * 2 + step) * vectors + group * SUB, SUB)
                    out[at, :] = source.own(layer, first + step, group)
                at = pl.ds(layers * 2 * vectors + layer * 2 + step, 1)
                out[at, :] = source.own(layer, first + step, source.groups)[:1]
        out[pl.ds(layers * 2 * (vectors + 1), SUB - layers * 2), :] = jnp.zeros((SUB - layers * 2, columns), jnp.float32)


class Fields:
    pass


def base_weights(at, other, layer):
    c = coupling_pair[layer]
    a = 1.0 / (4.0 + c)
    j = 0.25 * time_step
    pv_dx = at.near_dx - (4.0 + c) * at.dx + c * other.dx
    pv_dy = at.near_dy - (4.0 + c) * at.dy + c * other.dy
    return (
        j * (at.dy + a * pv_dy),
        -j * (at.dx + a * pv_dx),
        (j * a * a) * pv_dy,
        (-j * a * a) * pv_dx,
    )


def stepped(at, other, layer, weights):
    c, c_other = coupling_pair[layer], coupling_pair[1 - layer]
    cross = c * (4.0 + c) / (4.0 + c_other)
    v = time_step * hyper_visc
    result = (1.0 - 20.0 * v) * at.value + (8.0 * v) * at.near - (2.0 * v) * at.diagonal - v * at.far
    result = result + (weights[0] * at.dx + weights[1] * at.dy)
    result = result + weights[2] * (at.near_dx + cross * other.dx)
    return result + weights[3] * (at.near_dy + cross * other.dy)


def gram_of(whole, scale):
    return lax.dot_general(
        whole, whole, (((1,), (1,)), ((), ())),
        precision=lax.Precision.HIGHEST, preferred_element_type=jnp.float32,
    ) * scale


def at_end(part, columns):
    return jnp.concatenate([jnp.zeros((SUB, columns - part.shape[1]), jnp.float32), part], axis=1)


def tile_fields(source, group, wanted, edge_rows, edges):
    layers, columns = source.layers, source.columns
    place = lanes_of((SUB, columns)) // SPAN
    value, dx, sx, dx2, sx2 = {}, {}, {}, {}, {}
    spread = sorted({row + n for row in wanted for n in range(-2, 3)} | set(edge_rows))
    beside = {row + n for row in wanted for n in range(-1, 2)}
    for layer in range(layers):
        packed = edges(layer, None)
        for row in spread:
            here = source.get(layer, row, group)
            value[layer, row] = here
            if row in edge_rows:
                turned = pltpu.roll(here, (EDGE + SPAN * (row + 2)) % columns, 1)
                packed = jnp.where(place == row + 2, turned, packed)
            if row in beside:
                west, east = pltpu.roll(here, 1, 1), pltpu.roll(here, columns - 1, 1)
                dx[layer, row], sx[layer, row] = east - west, east + west
            if row in wanted:
                west, east = pltpu.roll(here, 2, 1), pltpu.roll(here, columns - 2, 1)
                dx2[layer, row], sx2[layer, row] = east - west, east + west
        edges(layer, packed)
    found = {}
    for layer in range(layers):
        for row in wanted:
            up, down = (layer, row - 1), (layer, row + 1)
            at = found[layer, row] = Fields()
            at.value, at.dx = value[layer, row], dx[layer, row]
            at.dy = value[down] - value[up]
            at.near = sx[layer, row] + (value[down] + value[up])
            at.near_dx = dx2[layer, row] + (dx[down] + dx[up])
            at.near_dy = (sx[down] - sx[up]) + (value[layer, row + 2] - value[layer, row - 2])
            at.diagonal = sx[down] + sx[up]
            at.far = sx2[layer, row] + (value[layer, row + 2] + value[layer, row - 2])
    return found


def step_rows(source, wanted, edge_rows, edges_of, evolved, coef):
    lane = lanes_of((SUB, source.columns))
    inside = jnp.logical_and(lane >= 2, lane < source.columns - 2)
    order = [source.groups, *range(source.groups)]
    for group in order:
        found = tile_fields(source, group, wanted, edge_rows, edges_of(group))
        for layer in range(source.layers):
            for n, row in enumerate(wanted):
                at = layer * len(wanted) + n
                here, other = found[layer, row], found[1 - layer, row]
                if group == source.groups:
                    for w, weight in enumerate(base_weights(here, other, layer)):
                        coef[at, w] = weight
                    continue
                result = stepped(here, other, layer, [coef[at, w] for w in range(4)])
                block = pl.ds(group * SUB, SUB), pl.ds(at * source.columns, source.columns)
                evolved[block] = jnp.where(inside, result, 0.0)


def edge_place(sizes, layer, group):
    vectors, layers = sizes[:2]
    if group < vectors // SUB:
        return pl.ds(layer * vectors + group * SUB, SUB)
    return pl.ds(layers * vectors + layer, 1)


def row_sets(rows):
    return tuple(range(2, rows - 2)), (0, 1), (rows - 2, rows - 1)


def rows_body(sizes, scale, wanted, edge_rows, below_only, pv, base, *refs):
    vectors, layers, _, columns = sizes
    refs = list(refs)
    halo = refs.pop(0) if below_only is not None else None
    before = [refs.pop(0), refs.pop(0)] if below_only is not None else None
    evolved, gram, edges, coef = refs if below_only is not True else (refs[0], None, refs[1], refs[2])
    source = Rows(sizes, pv, base, halo, halo)

    def edges_of(group):
        def put(layer, packed):
            at = edge_place(sizes, layer, group)
            if packed is not None:
                edges[at, :] = packed[: at.size]
            elif before is None:
                return jnp.zeros((SUB, columns), jnp.float32)
            else:
                return jnp.broadcast_to(before[1][at, :], (SUB, columns))

        return put

    step_rows(source, wanted, edge_rows, edges_of, evolved, coef)
    edges[pl.ds(layers * (vectors + 1), SUB - layers), :] = jnp.zeros((SUB - layers, columns), jnp.float32)
    local = gram_of(evolved[...], scale)
    for first in range(0, vectors, SUB):
        at = pl.ds(first, SUB)
        total = at_end(local[first : first + SUB], columns)
        if before is not None:
            total = before[0][at, :] + total
        if gram is not None:
            gram[at, :] = total
        else:
            edges[at, :] = edges[at, :] + total


def strip_fields(here, columns):
    turn = lambda value, by: pltpu.roll(value, by % columns, 1)
    at = Fields()
    west, east = turn(here, 1), turn(here, -1)
    at.value, at.dx, sx = here, east - west, east + west
    west, east = turn(here, 2), turn(here, -2)
    dx2, sx2 = east - west, east + west
    up, down = turn(here, SPAN), turn(here, -SPAN)
    at.dy, at.near = down - up, sx + (down + up)
    at.near_dx = dx2 + (turn(at.dx, -SPAN) + turn(at.dx, SPAN))
    far_up, far_down = turn(here, 2 * SPAN), turn(here, -2 * SPAN)
    sx_up, sx_down = turn(sx, SPAN), turn(sx, -SPAN)
    at.near_dy = (sx_down - sx_up) + (far_down - far_up)
    at.diagonal, at.far = sx_down + sx_up, sx2 + (far_down + far_up)
    return at


def join_body(sizes, scale, half, last, *refs):
    vectors, layers, rows, columns = sizes
    refs = list(refs)
    mine, got = refs[:2]
    sides_in = refs[2] if half > 1 else None
    outs = refs[3:] if half > 1 else refs[2:]
    message, sides, strips = outs
    groups = vectors // SUB
    shape = (SUB, columns)
    lane = lanes_of(shape)
    column = lax.rem(lane, SPAN)
    west_half = column < EDGE
    valid = jnp.logical_and(
        jnp.logical_and(column >= 2, column < SPAN - 2),
        jnp.logical_and(lane >= 2 * SPAN, lane < (rows + 2) * SPAN),
    )
    tile = lax.axis_index("gx")
    spot = lax.rem(tile, 2 * half)
    first = spot < half
    mid_mine = jnp.logical_xor(west_half, jnp.logical_not(first))
    keep_mid = jnp.logical_or(jnp.logical_and(west_half, spot == half - 1), jnp.logical_and(~west_half, spot == half))
    keep_wrap = jnp.logical_or(jnp.logical_and(west_half, spot == 2 * half - 1), jnp.logical_and(~west_half, spot == 0))
    kinds = (False, True) if last else (False,)
    weights = {}
    parcel = {}
    for group in (groups, *range(groups)):
        found = {}
        for layer in range(layers):
            at = edge_place(sizes, layer, group)
            here, there = mine[at, :], got[at, :]
            if group < groups and layer == 0:
                parcel[group] = here + there
            here, there = jnp.broadcast_to(here, shape), jnp.broadcast_to(there, shape)
            mid, outer = jnp.where(mid_mine, here, there), jnp.where(mid_mine, there, here)
            if not last:
                message[at, :] = outer[: at.size]
            found[layer, False] = strip_fields(mid, columns)
            if last:
                found[layer, True] = strip_fields(outer, columns)
        for layer in range(layers):
            own = None
            for wrap in kinds:
                at, other = found[layer, wrap], found[1 - layer, wrap]
                if group == groups:
                    weights[layer, wrap] = base_weights(at, other, layer)
                    continue
                result = jnp.where(valid, stepped(at, other, layer, weights[layer, wrap]), 0.0)
                strips[pl.ds(group * SUB, SUB), pl.ds((layer * len(kinds) + wrap) * columns, columns)] = result
                where = pl.ds(layer * vectors + group * SUB, SUB)
                if own is None:
                    own = sides_in[where, :] if half > 1 else jnp.zeros(shape, jnp.float32)
                own = jnp.where(keep_wrap if wrap else keep_mid, result, own)
                if wrap == last:
                    sides[where, :] = own
    if not last:
        message[pl.ds(layers * (vectors + 1), SUB - layers), :] = jnp.zeros((SUB - layers, columns), jnp.float32)
    local = gram_of(strips[...], scale)
    free = columns - vectors
    if last:
        total = jnp.zeros(shape, jnp.float32)
        for group in range(groups):
            turned = pltpu.roll(parcel[group], vectors * (group + 1) % columns, 1)
            total = jnp.where(lane // vectors == group, turned, total)
        packed = jnp.concatenate([local[at : at + SUB] for at in range(0, vectors, SUB)], axis=1)
        message[...] = total + packed
    else:
        for group in range(groups):
            block = pl.ds(group * SUB, SUB)
            joined = parcel[group] + at_end(local[group * SUB : (group + 1) * SUB], columns)
            message[block, :] = jnp.where(lane >= free, joined, message[block, :])


def ready_body(sizes, middle, upper_rows, lower_rows, sides, parts):
    vectors, layers, rows, columns = sizes
    lane = lanes_of((SUB * 2, columns))
    at_edge = jnp.logical_or(lane < 2, lane >= columns - 2)
    sets = row_sets(rows)
    pair = 2 * SUB
    for layer in range(layers):
        for row in range(rows):
            which = [row in part for part in sets].index(True)
            block = layer * len(sets[which]) + sets[which].index(row)
            for first in range(0, vectors, pair):
                edge = sides[pl.ds(layer * vectors + first, pair), :]
                edge = pltpu.roll(edge, -(SPAN * (row + 2) + EDGE) % columns, 1)
                here = (middle, upper_rows, lower_rows)[which][pl.ds(first, pair), pl.ds(block * columns, columns)]
                rest = jnp.where(at_edge, edge, here)
                for n in range(3):
                    part = rest.astype(jnp.bfloat16)
                    if n < 2:
                        rest = rest - part.astype(jnp.float32)
                    parts[pl.ds(n * vectors + first, pair), pl.ds((layer * rows + row) * columns, columns)] = part


def basis_body(sizes, parts, gram, basis, upper):
    vectors, layers, rows, columns = sizes
    groups = vectors // SUB
    shape = (SUB, columns)
    lane = lanes_of(shape)
    sub = lax.broadcasted_iota(jnp.int32, shape, 0)
    packed = gram[...]
    work = []
    for group in range(groups):
        turned = pltpu.roll(packed, (columns - group * vectors) % columns, 1)
        unit = jnp.where(lane - vectors == sub + group * SUB, 1.0, 0.0)
        work.append(jnp.where(lane < vectors, turned, unit))
    order = ((0, 0), (1, 0), (2, 0), (0, 1), (1, 1), (0, 2))
    per = columns // vectors
    inverse = []
    column = {}

    def spread(panel, above):
        for j in range(panel * SUB, (panel + 1) * SUB):
            for group in range(above, groups):
                column[group, j] = jnp.broadcast_to(work[group][:, j : j + 1], shape)

    spread(0, 0)
    for home in range(groups):
        if home + 1 < groups:
            spread(home + 1, home)
        root = jnp.ones(shape, jnp.float32)
        for at in range(SUB):
            k = home * SUB + at
            inverse_pivot = jnp.broadcast_to((1.0 / column[home, k])[at : at + 1, :], shape)
            line = jnp.broadcast_to(work[home][at : at + 1, :], shape)
            root = jnp.where(sub == at, column[home, k], root)
            factor = {group: column[group, k] * inverse_pivot for group in range(home, groups)}
            factor[home] = jnp.where(sub > at, factor[home], 0.0)
            for j in range(k + 1, min((home + 2) * SUB, vectors)):
                level = jnp.broadcast_to(column[home, j][at : at + 1, :], shape)
                for group in range(home, groups):
                    column[group, j] = column[group, j] - factor[group] * level
            for group in range(home, groups):
                work[group] = work[group] - factor[group] * line
        scaled = work[home] * (1.0 / jnp.sqrt(root))
        upper[pl.ds(home * SUB, SUB), :] = jnp.where(lane >= sub + home * SUB, scaled, 0.0)[:, :vectors]
        rest, terms = jnp.where(lane // vectors == 1, scaled, 0.0), []
        for _ in range(3):
            term = rest.astype(jnp.bfloat16).astype(jnp.float32)
            rest = rest - term
            terms.append(term)
        wide = []
        for first in range(0, len(order), per):
            line = jnp.zeros(shape, jnp.float32)
            for n, (mine, _) in enumerate(order[first : first + per]):
                line = line + pltpu.roll(terms[mine], (n - 1) * vectors % columns, 1)
            wide.append(line)
        inverse.append(jnp.concatenate(wide, axis=1))
    inverse = jnp.concatenate(inverse, axis=0).astype(jnp.bfloat16)[:, : len(order) * vectors]
    wide = 2 if rows % 2 == 0 else 1
    flat = basis
    stride = layers * rows
    for first in range(0, stride, wide):
        at = pl.ds(first * columns, wide * columns)
        split = [parts[pl.ds(n * vectors, vectors), at] for n in range(3)]
        part = jnp.dot(
            inverse, jnp.concatenate([split[n] for _, n in order], axis=0), preferred_element_type=jnp.float32
        )
        for n in range(wide):
            for group in range(groups):
                at = pl.ds(group * SUB * stride + first + n, SUB, stride=stride)
                flat[at, :] = part[group * SUB : (group + 1) * SUB, n * columns : (n + 1) * columns]


def exchange(value, axis, partner):
    count = lax.axis_size(axis)
    return lax.ppermute(value, axis, [(i, partner(i)) for i in range(count)])


def local(base_stream, tangent_vectors):
    sizes = tangent_vectors.shape
    vectors, layers, rows, columns = sizes
    down, across = lax.axis_size("gy"), lax.axis_size("gx")
    assert layers == 2 and down & (down - 1) == 0 and across & (across - 1) == 0 and across > 1
    assert rows >= 5 and (rows + 4) * SPAN + vectors <= columns and vectors * vectors == SUB * columns
    assert vectors % (2 * SUB) == 0
    pv = tangent_vectors.reshape(vectors * layers * rows, columns)
    base = base_stream.reshape(layers * rows, columns)
    f32 = lambda *shape: jax.ShapeDtypeStruct(shape, jnp.float32)

    def call(body, outs, *operands, scratch=(), inputs=VMEM, first_out=VMEM):
        return pl.pallas_call(
            lambda *refs: body(sizes, *refs),
            out_shape=outs,
            in_specs=[inputs] * len(operands),
            out_specs=[first_out] + [VMEM] * (len(outs) - 1),
            scratch_shapes=scratch,
            compiler_params=pltpu.CompilerParams(vmem_limit_bytes=8 << 20),
        )(*operands)

    strip = f32(layers * 2 * vectors + SUB, columns)
    bottom, top = call(
        pack_rows_body, [strip, strip],
        pltpu.with_memory_space_constraint(tangent_vectors.reshape(vectors * layers, rows, columns), pltpu.HBM),
        pltpu.with_memory_space_constraint(base, pltpu.HBM),
        inputs=pl.BlockSpec(memory_space=pltpu.HBM),
        scratch=[
            pltpu.VMEM((vectors * layers, rows, columns), jnp.float32),
            pltpu.VMEM((layers * rows, columns), jnp.float32),
            pltpu.SemaphoreType.DMA((3,)),
        ],
    )
    above = exchange(bottom, "gy", lambda i: (i + 1) % down)
    below = exchange(top, "gy", lambda i: (i - 1) % down)
    cells = layers * rows * columns
    scale = 1.0 / (cells * down * across)
    parcel = f32(layers * vectors + SUB, columns)
    middle_set, upper_set, lower_set = row_sets(rows)

    def rows_call(wanted, edge_rows, below_only, *operands):
        blocks = layers * len(wanted)
        return call(
            lambda sizes, *refs: rows_body(sizes, scale, wanted, edge_rows, below_only, *refs),
            [f32(vectors, blocks * columns)] + [f32(vectors, columns)] * (below_only is not True) + [parcel],
            pv, base, *operands,
            scratch=[pltpu.VMEM((blocks, 4, SUB, columns), jnp.float32)],
        )

    middle, gram, edges = rows_call(middle_set, range(rows), None)
    upper_rows, gram, edges = rows_call(upper_set, (-2, -1), False, above, gram, edges)
    lower_rows, message = rows_call(lower_set, (rows, rows + 1), True, below, gram, edges)
    half, sides = 1, ()
    while half < across:
        last = 2 * half == across
        got = exchange(message, "gx", lambda i: i ^ (2 * half - 1))
        body = lambda sizes, *refs, half=half, last=last: join_body(sizes, scale, half, last, *refs)
        message, *sides = call(
            body,
            [f32(SUB, columns) if last else parcel, f32(layers * vectors, columns)],
            message, got, *sides,
            scratch=[pltpu.VMEM((vectors, (2 if last else 1) * layers * columns), jnp.float32)],
        )
        half *= 2
    (parts,) = call(ready_body, [jax.ShapeDtypeStruct((3 * vectors, cells), jnp.bfloat16)], middle, upper_rows, lower_rows, *sides)
    gram = message
    half = 1
    while half < down:
        got = exchange(gram, ("gy", "gx"), lambda i: ((i // across) ^ half) * across + ((i % across) ^ 1))
        gram = gram + got
        half *= 2
    basis, upper = call(
        basis_body, [f32(vectors * layers * rows, columns), f32(vectors, vectors)], parts, gram
    )
    return basis.reshape(sizes), upper


def solution(mesh):
    return jax.shard_map(
        local,
        mesh=mesh,
        in_specs=(P("ens", "gy", "gx"), P("ens", None, "gy", "gx")),
        out_specs=(P("ens", None, "gy", "gx"), P("ens", None)),
        check_vma=False,
    )
```
